128 devices in a mesh: frames: 32 (over y, x, core), expert: 4 (over z).
Axes of the slice: x: 4, y: 4, z: 4, core: 2. Of those that a mesh axis runs over, the one named last changes fastest.
Arguments:
- residual: bfloat16 [32, 512, 1152], P('frames', 'expert'), may hold values from -6 to 6
- queries: bfloat16 [32, 512, 1152], P('frames', 'expert'), may hold values from -8 to 8
- keys_in: bfloat16 [32, 512, 1152], P('frames', 'expert'), may hold values from -8 to 8
- values: bfloat16 [32, 512, 1152], P('frames', 'expert'), may hold values from -6 to 6
- w_out: bfloat16 [1152, 1152], replicated, may hold values from -0.1875 to 0.1875
- norm_gain: float32 [1152], replicated, may hold values from 0.5 to 2
- w_router: bfloat16 [1152, 64], replicated, may hold values from -0.1875 to 0.1875
- routes: int32 [4, 32, 128, 2], P('expert', 'frames'), may hold values from 0 to 63, all different within a row; in each aligned block of 128 rows (0 to 127, 128 to 255, ..., all dimensions but the last counted through in order) at most 8 rows name the same one
- w_gate: bfloat16 [128, 1152, 512], P(('frames', 'expert')), may hold values from -0.1875 to 0.1875
- w_up: bfloat16 [128, 1152, 512], P(('frames', 'expert')), may hold values from -0.1875 to 0.1875
- w_down: bfloat16 [128, 512, 1152], P(('frames', 'expert')), may hold values from -0.1875 to 0.1875
- d_out: bfloat16 [32, 512, 1152], P('frames', 'expert'), may hold values from -2 to 2
Outputs:
- block_out: bfloat16 [32, 512, 1152], P('frames', 'expert')
- d_hidden: bfloat16 [32, 512, 1152], P('frames', 'expert')
- d_gate: float32 [128, 1152, 512], P(('frames', 'expert'))
- d_up: float32 [128, 1152, 512], P(('frames', 'expert'))
- d_down: float32 [128, 512, 1152], P(('frames', 'expert'))
The draws below stay inside these ranges and needn't reach their ends.
Inputs may be any that keep to these rules, and one draw needn't show every extreme that they name: `routes`: the two experts of a token differ. In the rows of one device (the aligned blocks of 128 rows over the flattened leading dimensions) no expert is named more than 8 times; some expert is named exactly 8 times in some of these blocks.
All inputs are finite; a program needn't handle non-finite values.
Results may differ from the reference program's by a relative error of at most 0.018.
Values may be sent and summed in bfloat16 or wider, within the bound.
No kernel may reach another device: no remote copies, remote signals or barrier semaphores. Data moves between devices by JAX's collectives and lax.ppermute only.
A program may use at most 128 MiB of HBM per device.

```python
import math
import jax
import jax.numpy as jnp
import numpy as np
from jax import lax

D = 1152
H = 16
FF = 1024
P_SIZE = 512
FFH = 512
F = 32
GROUPS = 4
PQ = 128
TOK_DEV = 128
EXPERTS = 64
CAP = 8
DEVICES = 128


def attention_pair(key):
    base = jax.random.fold_in(key, 11)
    streams = jax.random.split(base, 2)
    queries = jnp.clip(jax.random.normal(streams[0], (F, P_SIZE, D), jnp.float32), -8.0, 8.0)
    keys_out = jnp.clip(jax.random.normal(streams[1], (F, P_SIZE, D), jnp.float32), -8.0, 8.0)
    return (queries, keys_out)


def draw_queries(key, part):
    return attention_pair(key)[0].astype(jnp.bfloat16)


def draw_keys_in(key, part):
    return attention_pair(key)[1].astype(jnp.bfloat16)


def block_scale(own_key, shape, cuts, least, largest):
    factor_of, own = 1.0, jax.random.fold_in(own_key, 6)
    for axis_at, parts in cuts:
        steps = jnp.exp(jax.random.uniform(jax.random.fold_in(own, axis_at), (parts,), jnp.float32, least / len(cuts), largest / len(cuts)))
        factor_of = factor_of * jnp.repeat(steps, shape[axis_at] // parts).reshape([-1 if axis == axis_at else 1 for axis in range(len(shape))])
    return factor_of


def assign_block(rng, own, number, rows, count, top, limit, slope):
    sequence = jax.random.permutation(rng, count)
    crowded, common = load_shares(count, rows * top, limit, slope, True), load_shares(count, rows * top, limit, slope, False)
    places = jnp.arange(count)

    def named(tallies, turn):
        used = int((tallies > 0).sum())
        fixed = max(1, used // 4)
        passed = fixed + (places - fixed + turn * (used - fixed)) % max(1, count - fixed)
        return jnp.zeros((count,), jnp.int32).at[sequence[jnp.where(places < fixed, places, passed)]].set(jnp.asarray(tallies, jnp.int32))

    tallies = jnp.where(number % 4 == 0, named(crowded, number // 4), named(common, number - number // 4 - 1))
    mixed = jax.random.permutation(jax.random.fold_in(own, 3), count)
    source_of, sink = mixed[0:count // 2 * 2:2], mixed[1:count // 2 * 2:2]
    slack = jnp.minimum(tallies[source_of] - 1, limit - tallies[sink]) // 2
    slack = jnp.where((source_of == sequence[0]) | (sink == sequence[0]) | (tallies[sink] == 0), 0, jnp.maximum(slack, 0))
    passed = jax.random.randint(jax.random.fold_in(own, 4), (count // 2,), 0, 1 << 20) % (slack + 1)
    tallies = tallies.at[source_of].add(-passed).at[sink].add(passed)
    members = jnp.searchsorted(jnp.cumsum(tallies), jnp.arange(rows * top), side="right").astype(jnp.int32)
    table = members.reshape(top, rows).T
    table = table[jax.random.permutation(jax.random.fold_in(own, 1), rows)]
    turn = jax.random.randint(jax.random.fold_in(own, 2), (rows, 1), 0, top)
    return jnp.take_along_axis(table, (jnp.arange(top)[None, :] + turn) % top, axis=1)


def load_shares(count, total, limit, slope, full):
    portions = [(1 << 20) // math.isqrt(rank ** slope) + 1 for rank in range(1, count + 1)]
    largest = limit if full else min(limit, max(-(-total // count), total * portions[0] // sum(portions)))
    least = 1 if total - largest >= count - 1 else 0
    holding, spare = [largest] + [least] * (count - 1), total - largest - least * (count - 1)
    while spare > 0:
        movable = [i for i in range(1, count) if holding[i] < largest] or [i for i in range(1, count) if holding[i] < limit]
        whole, remaining = sum([portions[i] for i in movable]), spare
        for i in movable:
            more = min(limit - holding[i], max(1, remaining * portions[i] // whole), spare)
            holding[i] = holding[i] + more
            spare = spare - more
    return np.array(holding)


def gaussian(own_key, extent, deviation, limit, shards=(), kind=jnp.bfloat16):
    entries = deviation * jax.random.normal(own_key, extent, jnp.float32)
    if shards:
        entries = entries * block_scale(own_key, extent, shards, -0.22, 0.18)
    return jnp.clip(entries, -limit, limit).astype(kind)


def setup_inputs(seed: int = 0) -> dict:
    keys = jax.random.split(jax.random.key(seed), 13)
    residual = gaussian(keys[0], (F, P_SIZE, D), 1.0, 6.0, ((0, 32), (1, 4)))
    queries = draw_queries(jax.random.fold_in(keys[12], 71), 0)
    keys_in = draw_keys_in(jax.random.fold_in(keys[12], 71), 0)
    values = gaussian(keys[3], (F, P_SIZE, D), 1.0, 6.0, ((0, 32), (1, 4)))
    w_out = gaussian(keys[4], (D, D), D ** -0.5, 0.1875)
    norm_gain = jnp.clip(jnp.exp(jax.random.uniform(keys[5], (D,), jnp.float32, math.log(0.5), math.log(2.0))), 0.5, 2.0)
    w_router = gaussian(keys[6], (D, EXPERTS), D ** -0.5, 0.1875)
    routes_keys = jax.random.split(jax.random.fold_in(keys[7], 1), GROUPS * F * PQ // TOK_DEV)
    routes_turns = jax.random.permutation(jax.random.fold_in(keys[7], 3), GROUPS * F * PQ // TOK_DEV)
    routes = jax.vmap(lambda own, number: assign_block(jax.random.fold_in(keys[7], 2), own, number, TOK_DEV, EXPERTS, 2, CAP, 2))(routes_keys, routes_turns).reshape((GROUPS, F, PQ, 2))
    w_gate = gaussian(keys[8], (2 * EXPERTS, D, FFH), D ** -0.5, 0.1875, ((0, 128),))
    w_up = gaussian(keys[9], (2 * EXPERTS, D, FFH), D ** -0.5, 0.1875, ((0, 128),))
    w_down = gaussian(keys[10], (2 * EXPERTS, FFH, D), FF ** -0.5, 0.1875, ((0, 128),))
    d_out = gaussian(keys[11], (F, P_SIZE, D), 0.25, 2.0, ((0, 32), (1, 4)))
    return {"residual": residual, "queries": queries, "keys_in": keys_in, "values": values, "w_out": w_out, "norm_gain": norm_gain, "w_router": w_router, "routes": routes, "w_gate": w_gate, "w_up": w_up, "w_down": w_down, "d_out": d_out}


def expert_pass(normed_rows, scaled_rows):

    def run(operands):
        rows, gate_pair, up_pair, down_pair = operands
        inputs_in = normed_rows[rows]
        grad_in = scaled_rows[rows]
        expert_sum = jnp.zeros((rows.shape[0], inputs_in.shape[1]), jnp.float32)
        input_sum = jnp.zeros((rows.shape[0], inputs_in.shape[1]), jnp.float32)
        gate_grads = []
        up_grads = []
        down_grads = []
        for half_idx in range(2):
            gate_w = gate_pair[half_idx]
            up_w = up_pair[half_idx]
            down_w = down_pair[half_idx]
            pre_gate = jnp.dot(inputs_in, gate_w, preferred_element_type=jnp.float32)
            pre_up = jnp.dot(inputs_in, up_w, preferred_element_type=jnp.float32)
            gate_sig = jax.nn.sigmoid(pre_gate)
            gate_act = pre_gate * gate_sig
            hidden_units = (gate_act * pre_up).astype(jnp.bfloat16)
            part_out = jnp.dot(hidden_units, down_w, preferred_element_type=jnp.float32).astype(jnp.bfloat16)
            expert_sum = expert_sum + lax.optimization_barrier(part_out).astype(jnp.float32)
            d_units = jnp.dot(grad_in, down_w.T, preferred_element_type=jnp.float32)
            d_pre_gate = (d_units * pre_up * (gate_sig + pre_gate * gate_sig * (1.0 - gate_sig))).astype(jnp.bfloat16)
            d_pre_up = (d_units * gate_act).astype(jnp.bfloat16)
            down_grads.append(jnp.dot(hidden_units.T, grad_in, preferred_element_type=jnp.float32))
            gate_grads.append(jnp.dot(inputs_in.T, d_pre_gate, preferred_element_type=jnp.float32))
            up_grads.append(jnp.dot(inputs_in.T, d_pre_up, preferred_element_type=jnp.float32))
            part_in = (jnp.dot(d_pre_gate, gate_w.T, preferred_element_type=jnp.float32) + jnp.dot(d_pre_up, up_w.T, preferred_element_type=jnp.float32)).astype(jnp.bfloat16)
            input_sum = input_sum + lax.optimization_barrier(part_in).astype(jnp.float32)
        expert_sum = lax.optimization_barrier(expert_sum.astype(jnp.bfloat16)).astype(jnp.float32)
        input_sum = lax.optimization_barrier(input_sum.astype(jnp.bfloat16)).astype(jnp.float32)
        return (expert_sum, input_sum, jnp.stack(gate_grads), jnp.stack(up_grads), jnp.stack(down_grads))
    return run

def reference(residual, queries, keys_in, values, w_out, norm_gain, w_router, routes, w_gate, w_up, w_down, d_out):
    head_width = D // H

    def heads_view(tensor):
        return tensor.astype(jnp.float32).reshape(F, P_SIZE, H, head_width)
    scores = jnp.einsum('fphd,gphd->phfg', heads_view(queries), heads_view(keys_in), precision=lax.Precision.HIGHEST) * head_width ** (-0.5)
    row_peak = lax.optimization_barrier(jnp.max(scores, axis=-1, keepdims=True))
    weights = jnp.exp(scores - row_peak)
    attn_probs = (weights / lax.optimization_barrier(jnp.sum(weights, axis=-1, keepdims=True))).astype(jnp.bfloat16)
    attended = jnp.einsum('phfg,gphd->fphd', attn_probs.astype(jnp.float32), heads_view(values), precision=lax.Precision.HIGHEST).astype(jnp.bfloat16)
    tok_total = F * P_SIZE
    attended = attended.reshape(tok_total, D)
    stream = residual.reshape(tok_total, D).astype(jnp.float32) + jnp.dot(attended, w_out, preferred_element_type=jnp.float32)
    hidden = stream.astype(jnp.bfloat16)
    hidden_float = hidden.astype(jnp.float32)
    inv_rms = lax.rsqrt(lax.optimization_barrier(jnp.mean(hidden_float * hidden_float, axis=-1, keepdims=True)) + 1e-06)
    normed = (hidden_float * inv_rms * norm_gain).astype(jnp.bfloat16)
    logits = jnp.dot(normed, w_router, preferred_element_type=jnp.float32)
    picked = jnp.transpose(routes, (1, 0, 2, 3)).reshape(tok_total, 2)
    onehot = picked[:, :, None] == jnp.arange(EXPERTS, dtype=jnp.int32)[None, None, :]
    chosen = lax.optimization_barrier(jnp.sum(jnp.where(onehot, logits[:, None, :], 0.0), axis=-1))
    combine = jax.nn.sigmoid(chosen)
    cotangent = d_out.reshape(tok_total, D).astype(jnp.float32)
    scaled = (combine[:, :, None] * cotangent[:, None, :]).astype(jnp.bfloat16)
    assign_total = 2 * tok_total
    flag_rows = onehot.reshape(assign_total, EXPERTS).astype(jnp.int32)
    before = jnp.cumsum(flag_rows, axis=0) - flag_rows
    ranking = lax.optimization_barrier(jnp.sum(before * flag_rows, axis=-1)).astype(jnp.int32)
    expert_ids = picked.reshape(-1).astype(jnp.int32)
    bound_rows = DEVICES * CAP
    table = jnp.full((EXPERTS, bound_rows), assign_total, jnp.int32)
    table = table.at[expert_ids, ranking].set(jnp.arange(assign_total, dtype=jnp.int32))
    normed_rows = jnp.concatenate([jnp.repeat(normed, 2, axis=0), jnp.zeros((1, D), jnp.bfloat16)], axis=0)
    scaled_rows = jnp.concatenate([scaled.reshape(assign_total, D), jnp.zeros((1, D), jnp.bfloat16)], axis=0)
    expert_sums, input_sums, gate_grads, up_grads, down_grads = lax.map(expert_pass(normed_rows, scaled_rows), (table, w_gate.reshape(EXPERTS, 2, D, FF // 2), w_up.reshape(EXPERTS, 2, D, FF // 2), w_down.reshape(EXPERTS, 2, FF // 2, D)))
    flat_table = table.reshape(-1)
    expert_outs = jnp.zeros((assign_total + 1, D), jnp.float32).at[flat_table].set(expert_sums.reshape(-1, D))[:assign_total].reshape(tok_total, 2, D)
    d_routed = jnp.zeros((assign_total + 1, D), jnp.float32).at[flat_table].set(input_sums.reshape(-1, D))[:assign_total].reshape(tok_total, 2, D)
    block_sum = hidden_float + lax.optimization_barrier(jnp.sum(combine[:, :, None] * expert_outs, axis=1))
    block_out = block_sum.astype(jnp.bfloat16).reshape(F, P_SIZE, D)
    d_combine = lax.optimization_barrier(jnp.sum(cotangent[:, None, :] * expert_outs, axis=-1))
    d_logit = d_combine * combine * (1.0 - combine)
    router_rows = lax.optimization_barrier(jnp.sum(jnp.where(onehot, d_logit[:, :, None], 0.0), axis=1))
    d_normed = lax.optimization_barrier(jnp.sum(d_routed, axis=1)) + jnp.dot(router_rows, w_router.astype(jnp.float32).T, precision=lax.Precision.HIGHEST)
    gained = d_normed * norm_gain
    d_norm_in = inv_rms * gained - hidden_float * inv_rms ** 3 * lax.optimization_barrier(jnp.mean(gained * hidden_float, axis=-1, keepdims=True))
    d_hidden = (cotangent + d_norm_in).astype(jnp.bfloat16).reshape(F, P_SIZE, D)
    return (block_out, d_hidden, gate_grads.reshape(2 * EXPERTS, D, FF // 2), up_grads.reshape(2 * EXPERTS, D, FF // 2), down_grads.reshape(2 * EXPERTS, FF // 2, D))
```

```python
import jax
import jax.numpy as jnp
from jax import lax
from jax.experimental import pallas as pl
from jax.experimental.pallas import tpu as pltpu
from jax.sharding import PartitionSpec as P

H = 16
F32 = jnp.float32
BF16 = jnp.bfloat16
WIDE = 640
STEP = 512
LIMIT = 48 * 1024 * 1024


def call(body, outs, cost, **extra):
    flops, moved = cost
    return pl.pallas_call(
        body,
        out_shape=outs,
        compiler_params=pltpu.CompilerParams(vmem_limit_bytes=LIMIT),
        cost_estimate=pl.CostEstimate(flops=flops, bytes_accessed=moved, transcendentals=0),
        **extra,
    )


def shape(dims, dtype):
    return jax.ShapeDtypeStruct(dims, dtype)


def rows_of(blocks):
    n, eight, width = blocks.shape
    return blocks.astype(F32).reshape(n * eight, width)


def blocks_of(rows):
    total, width = rows.shape
    return rows.reshape(total // 8, 8, width).astype(BF16)


def pack_body(q_ref, k_ref, v_ref, out_ref):
    for s, ref in enumerate((q_ref, k_ref, v_ref)):
        for i in range(ref.shape[0] // 8):
            for half in range(2):
                out_ref[2 * i + half, 8 * s : 8 * s + 8, :] = ref[
                    8 * i : 8 * i + 8, STEP * half : STEP * half + WIDE
                ]


def pair_onehots(routes_ref, experts):
    tok = routes_ref.shape[0]
    lanes = lax.broadcasted_iota(jnp.int32, (tok, experts), 1)
    return [routes_ref[:, j : j + 1] == lanes for j in range(2)]


def to_slots(picks, rows, out_ref):
    slots = picks.shape[1]
    step = 128
    for at in range(0, slots, step):
        moved = lax.dot_general(
            picks[:, at : at + step], rows, (((0,), (0,)), ((), ())), preferred_element_type=F32
        )
        blocks = blocks_of(moved)
        out_ref[at // 8 : (at + step) // 8, 0] = blocks
        out_ref[at // 8 : (at + step) // 8, 1] = blocks


def route_body(experts, routes_ref, cot_ref, pick0_ref, pick1_ref, out_ref):
    tok = routes_ref.shape[0]
    slots = pick0_ref.shape[1]
    onehots = pair_onehots(routes_ref, experts)
    named = jnp.where(onehots[0] | onehots[1], 1.0, 0.0)
    earlier = lax.broadcasted_iota(jnp.int32, (tok, tok), 0) > lax.broadcasted_iota(
        jnp.int32, (tok, tok), 1
    )
    before = jnp.dot(
        jnp.where(earlier, 1.0, 0.0).astype(BF16), named.astype(BF16), preferred_element_type=F32
    )
    slot_lanes = lax.broadcasted_iota(jnp.int32, (tok, slots), 1)
    picks = []
    for j, ref in enumerate((pick0_ref, pick1_ref)):
        rank = jnp.sum(jnp.where(onehots[j], before, 0.0), axis=1, keepdims=True)
        slot = routes_ref[:, j : j + 1] * (slots // experts) + rank.astype(jnp.int32)
        pick = jnp.where(slot_lanes == slot, 1.0, 0.0)
        ref[...] = pick.astype(BF16)
        picks.append(pick)
    to_slots((picks[0] + picks[1]).astype(BF16), cot_ref[...], out_ref)


def attend_body(head_width, off_ref, qkv_ref, out_ref):
    frames = qkv_ref.shape[0]
    q, k, v = [rows_of(qkv_ref[:, 8 * s : 8 * s + 8, :]).astype(BF16) for s in range(3)]
    rows = frames * 8
    off = off_ref[0]
    same = (
        lax.broadcasted_iota(jnp.int32, (rows, rows), 0) & 7
    ) == (lax.broadcasted_iota(jnp.int32, (rows, rows), 1) & 7)
    lane = lax.broadcasted_iota(jnp.int32, (rows, 256), 1)
    tiles = [jnp.zeros((rows, 128), F32) for _ in range(WIDE // 128)]
    for h in range(H // 2):
        w = h // 2
        first = off + head_width * h - 128 * w
        inside = (lane >= first) & (lane < first + head_width)
        cols = slice(128 * w, 128 * w + 256)
        mine = jnp.where(inside, q[:, cols].astype(F32), 0.0).astype(BF16)
        scores = lax.dot_general(
            mine, k[:, cols], (((1,), (1,)), ((), ())), preferred_element_type=F32
        ) * head_width ** (-0.5)
        scores = jnp.where(same, scores, -1e30)
        peak = jnp.max(scores, axis=1, keepdims=True)
        weights = jnp.exp(scores - peak)
        probs = (weights / jnp.sum(weights, axis=1, keepdims=True)).astype(BF16)
        got = jnp.dot(probs, v[:, cols], preferred_element_type=F32)
        for t in range(2):
            part = slice(128 * t, 128 * t + 128)
            tiles[w + t] = jnp.where(inside[:, part], got[:, part], tiles[w + t])
    for t, tile in enumerate(tiles):
        out_ref[:, :, 128 * t : 128 * t + 128] = blocks_of(tile)


def inv_rms_of(hidden_float):
    return lax.rsqrt(jnp.mean(hidden_float * hidden_float, axis=-1, keepdims=True) + 1e-06)


def project_body(
    att_ref, residual_ref, w_out_ref, gain_ref, w_router_ref, routes_ref, pick0_ref, pick1_ref,
    hidden_ref, combine_ref, out_ref,
):
    low, high = rows_of(att_ref[:, 0]), rows_of(att_ref[:, 1])
    shared = WIDE - STEP
    attended = jnp.concatenate(
        [low[:, :STEP], low[:, STEP:] + high[:, :shared], high[:, shared:]], axis=1
    ).astype(BF16)
    stream = residual_ref[...].astype(F32) + jnp.dot(
        attended, w_out_ref[...], preferred_element_type=F32
    )
    hidden = stream.astype(BF16)
    hidden_ref[...] = hidden
    hidden_float = hidden.astype(F32)
    normed = (hidden_float * inv_rms_of(hidden_float) * gain_ref[...]).astype(BF16)
    to_slots(pick0_ref[...] + pick1_ref[...], normed, out_ref)
    logits = jnp.dot(normed, w_router_ref[...], preferred_element_type=F32)
    onehots = pair_onehots(routes_ref, w_router_ref.shape[1])
    for j in range(2):
        chosen = jnp.sum(jnp.where(onehots[j], logits, 0.0), axis=1, keepdims=True)
        combine_ref[:, j : j + 1] = jax.nn.sigmoid(chosen)


def forward_body(
    expert_ref, x_ref, cot_ref, w_router_ref, gate_ref, up_ref, down_ref,
    out_ref, scaled_ref, units_ref, slope_ref, act_ref,
):
    x = x_ref[...]
    pre_gate = jnp.dot(x, gate_ref[...], preferred_element_type=F32)
    pre_up = jnp.dot(x, up_ref[...], preferred_element_type=F32)
    gate_sig = jax.nn.sigmoid(pre_gate)
    gate_act = pre_gate * gate_sig
    units = (gate_act * pre_up).astype(BF16)
    out_ref[...] = jnp.dot(units, down_ref[...], preferred_element_type=F32).astype(BF16)
    units_ref[...] = units
    slope_ref[...] = pre_up * (gate_sig + gate_act * (1.0 - gate_sig))
    act_ref[...] = gate_act
    logits = jnp.dot(x, w_router_ref[...], preferred_element_type=F32)
    lanes = lax.broadcasted_iota(jnp.int32, logits.shape, 1)
    chosen = jnp.sum(jnp.where(lanes == expert_ref[0], logits, 0.0), axis=1, keepdims=True)
    scaled_ref[...] = (jax.nn.sigmoid(chosen) * cot_ref[...].astype(F32)).astype(BF16)


def backward_body(
    scaled_ref, slope_ref, act_ref, gate_ref, up_ref, down_ref, d_in_ref, d_gate_ref, d_up_ref
):
    turned = (((1,), (1,)), ((), ()))
    d_units = lax.dot_general(
        scaled_ref[...], down_ref[...], turned, preferred_element_type=F32
    )
    d_pre_gate = (d_units * slope_ref[...]).astype(BF16)
    d_pre_up = (d_units * act_ref[...]).astype(BF16)
    d_gate_ref[...] = d_pre_gate
    d_up_ref[...] = d_pre_up
    d_in_ref[...] = (
        lax.dot_general(d_pre_gate, gate_ref[...], turned, preferred_element_type=F32)
        + lax.dot_general(d_pre_up, up_ref[...], turned, preferred_element_type=F32)
    ).astype(BF16)


def pair_sum(ref):
    return (rows_of(ref[:, 0]) + rows_of(ref[:, 1])).astype(BF16)


def output_body(
    back_ref, pick0_ref, pick1_ref, combine_ref, cot_ref, hidden_ref, w_router_ref, routes_ref,
    block_ref, router_ref,
):
    summed = pair_sum(back_ref)
    cotangent = cot_ref[...].astype(F32)
    block = hidden_ref[...].astype(F32)
    onehots = pair_onehots(routes_ref, w_router_ref.shape[1])
    rows = jnp.zeros(onehots[0].shape, F32)
    for j, pick_ref in enumerate((pick0_ref, pick1_ref)):
        combine = combine_ref[:, j : j + 1]
        expert_out = jnp.dot(pick_ref[...], summed, preferred_element_type=F32)
        block = block + combine * expert_out
        d_combine = jnp.sum(cotangent * expert_out, axis=1, keepdims=True)
        rows = rows + jnp.where(onehots[j], d_combine * combine * (1.0 - combine), 0.0)
    block_ref[...] = block.astype(BF16)
    router_ref[...] = lax.dot_general(
        rows,
        w_router_ref[...].astype(F32),
        (((1,), (1,)), ((), ())),
        precision=lax.Precision.HIGHEST,
        preferred_element_type=F32,
    )


def input_body(back_ref, pick0_ref, pick1_ref, router_ref, hidden_ref, gain_ref, cot_ref, out_ref):
    picks = pick0_ref[...] + pick1_ref[...]
    d_normed = router_ref[...] + jnp.dot(picks, pair_sum(back_ref), preferred_element_type=F32)
    hidden_float = hidden_ref[...].astype(F32)
    inv_rms = inv_rms_of(hidden_float)
    gained = d_normed * gain_ref[...]
    d_norm_in = inv_rms * gained - hidden_float * inv_rms**3 * jnp.mean(
        gained * hidden_float, axis=-1, keepdims=True
    )
    out_ref[...] = (cot_ref[...].astype(F32) + d_norm_in).astype(BF16)


def relay(parcel, axes):
    return lax.all_to_all(parcel, axes, split_axis=0, concat_axis=0, tiled=True)


def on_device(
    residual, queries, keys_in, values, w_out, norm_gain, w_router, routes, w_gate, w_up, w_down,
    d_out,
):
    everyone = ("frames", "expert")
    frames = lax.axis_size("frames")
    devices = frames * lax.axis_size("expert")
    width = residual.shape[2]
    tok = residual.shape[0] * residual.shape[1]
    experts = w_router.shape[1]
    cap = 4 * tok // experts
    slots = experts * cap
    hidden_units = w_gate.shape[2]
    smem = pl.BlockSpec(memory_space=pltpu.SMEM)
    vmem = pl.BlockSpec(memory_space=pltpu.VMEM)
    flat = lambda a: a.reshape(tok, width)
    cot = flat(d_out)
    picked = routes.reshape(tok, 2)
    gain = norm_gain.reshape(1, width)
    me = lax.axis_index("frames")
    offset = (me % 2 * (width // 2 - STEP)).reshape(1)
    expert = ((me * lax.axis_size("expert") + lax.axis_index("expert")) // 2).reshape(1)

    packed = call(pack_body, shape((frames, 24, WIDE), BF16), (0, 2 * frames * 24 * WIDE * 2))(
        flat(queries), flat(keys_in), flat(values)
    )
    qkv = relay(packed, "frames")
    parcel = shape((experts, 2, cap, width), BF16)
    pick0, pick1, cot_out = call(
        lambda *refs: route_body(experts, *refs),
        (shape((tok, slots), BF16), shape((tok, slots), BF16), parcel),
        (2 * tok * slots * width, 3 * slots * width * 2),
    )(picked, cot)
    cot_in = relay(cot_out.reshape(devices, cap, width), everyone)
    attended = call(
        lambda *refs: attend_body(width // H, *refs),
        shape((frames, 8, WIDE), BF16),
        (1 << 29, 4 * frames * 8 * WIDE * 2),
        in_specs=[smem, vmem],
    )(offset, qkv)
    attended = relay(attended, "frames").reshape(frames // 2, 2, 8, WIDE)
    hidden, combine, outbound = call(
        project_body,
        (shape((tok, width), BF16), shape((tok, 2), F32), parcel),
        (2 * tok * width * (width + slots), (width + 3 * slots) * width * 2),
    )(attended, flat(residual), w_out, gain, w_router, picked, pick0, pick1)
    arrived = relay(outbound.reshape(devices, cap, width), everyone)

    total = devices * cap
    block = 256
    by_rows = lambda w: pl.BlockSpec((block, w), lambda i: (i, 0))
    whole = lambda a: pl.BlockSpec(a.shape, lambda i: (0, 0))
    gate_w, up_w, down_w = w_gate[0], w_up[0], w_down[0]
    x = arrived.reshape(total, width)
    product = 2 * total * width * hidden_units
    part_out, scaled, units, slope, act = call(
        forward_body,
        (
            shape((total, width), BF16),
            shape((total, width), BF16),
            shape((total, hidden_units), BF16),
            shape((total, hidden_units), F32),
            shape((total, hidden_units), F32),
        ),
        (3 * product, 8 * total * width * 2),
        grid=(total // block,),
        in_specs=[smem, by_rows(width), by_rows(width), whole(w_router), whole(gate_w),
                  whole(up_w), whole(down_w)],
        out_specs=[by_rows(width), by_rows(width)] + [by_rows(hidden_units)] * 3,
    )(expert, x, cot_in.reshape(total, width), w_router, gate_w, up_w, down_w)
    out_back = relay(part_out.reshape(devices, cap, width), everyone)
    part_in, d_pre_gate, d_pre_up = call(
        backward_body,
        (
            shape((total, width), BF16),
            shape((total, hidden_units), BF16),
            shape((total, hidden_units), BF16),
        ),
        (3 * product, 8 * total * width * 2),
        grid=(total // block,),
        in_specs=[by_rows(width), by_rows(hidden_units), by_rows(hidden_units), whole(gate_w),
                  whole(up_w), whole(down_w)],
        out_specs=[by_rows(width), by_rows(hidden_units), by_rows(hidden_units)],
    )(scaled, slope, act, gate_w, up_w, down_w)
    in_back = relay(part_in.reshape(devices, cap, width), everyone)
    d_down = jnp.dot(units.T, scaled, preferred_element_type=F32)
    d_gate = jnp.dot(x.T, d_pre_gate, preferred_element_type=F32)
    d_up = jnp.dot(x.T, d_pre_up, preferred_element_type=F32)

    pairs = (experts, 2, cap, width)
    block_out, router_part = call(
        output_body,
        (shape((tok, width), BF16), shape((tok, width), F32)),
        (4 * tok * width * slots, 4 * slots * width * 2),
    )(out_back.reshape(pairs), pick0, pick1, combine, cot, hidden, w_router, picked)
    d_hidden = call(
        input_body,
        shape((tok, width), BF16),
        (2 * tok * width * slots, 4 * slots * width * 2),
    )(in_back.reshape(pairs), pick0, pick1, router_part, hidden, gain, cot)
    return (
        block_out.reshape(residual.shape),
        d_hidden.reshape(residual.shape),
        d_gate[None],
        d_up[None],
        d_down[None],
    )


def solution(mesh):
    tokens = P("frames", "expert", None)
    weights = P(("frames", "expert"), None, None)
    return jax.shard_map(
        on_device,
        mesh=mesh,
        in_specs=(tokens,) * 4
        + (P(), P(), P(), P("expert", "frames", None, None))
        + (weights,) * 3
        + (tokens,),
        out_specs=(tokens, tokens, weights, weights, weights),
        check_vma=False,
    )
```

```python
import jax
import jax.numpy as jnp
from jax import lax
from jax.experimental import pallas as pl
from jax.experimental.pallas import tpu as pltpu
from jax.sharding import PartitionSpec as P

H = 16
F32 = jnp.float32
BF16 = jnp.bfloat16
WIDE = 640
STEP = 512
LIMIT = 48 * 1024 * 1024


def call(body, outs, cost, **extra):
    flops, moved = cost
    return pl.pallas_call(
        body,
        out_shape=outs,
        compiler_params=pltpu.CompilerParams(vmem_limit_bytes=LIMIT),
        cost_estimate=pl.CostEstimate(flops=flops, bytes_accessed=moved, transcendentals=0),
        **extra,
    )


def shape(dims, dtype):
    return jax.ShapeDtypeStruct(dims, dtype)


def rows_of(blocks):
    n, eight, width = blocks.shape
    return blocks.astype(F32).reshape(n * eight, width)


def blocks_of(rows):
    total, width = rows.shape
    return rows.reshape(total // 8, 8, width).astype(BF16)


def pair_onehots(routes_ref, experts):
    tok = routes_ref.shape[0]
    lanes = lax.broadcasted_iota(jnp.int32, (tok, experts), 1)
    return [routes_ref[:, j : j + 1] == lanes for j in range(2)]


def slot_rows(picks, rows, step, store):
    for at in range(0, picks.shape[1], step):
        moved = lax.dot_general(
            picks[:, at : at + step], rows, (((0,), (0,)), ((), ())), preferred_element_type=F32
        )
        store(at // 8, blocks_of(moved))


def pack_body(
    experts, mine_ref, routes_ref, cot_ref, q_ref, k_ref, v_ref,
    out_ref, pick0_ref, pick1_ref, held_ref, sems,
):
    copies = []
    for s, ref in enumerate((q_ref, k_ref, v_ref)):
        for half in range(2):
            copies.append(
                pltpu.make_async_copy(
                    ref.at[:, :, STEP * half : STEP * half + WIDE],
                    out_ref.at[:, half, :, WIDE * s : WIDE * s + WIDE],
                    sems.at[2 * s + half],
                )
            )
            copies[-1].start()
    tok, slots = pick0_ref.shape
    width = cot_ref.shape[1]
    onehots = pair_onehots(routes_ref, experts)
    named = jnp.where(onehots[0] | onehots[1], 1.0, 0.0)
    earlier = lax.broadcasted_iota(jnp.int32, (tok, tok), 0) > lax.broadcasted_iota(
        jnp.int32, (tok, tok), 1
    )
    before = jnp.dot(
        jnp.where(earlier, 1.0, 0.0).astype(BF16), named.astype(BF16), preferred_element_type=F32
    )
    slot_lanes = lax.broadcasted_iota(jnp.int32, (tok, slots), 1)
    picks = []
    for j, ref in enumerate((pick0_ref, pick1_ref)):
        rank = jnp.sum(jnp.where(onehots[j], before, 0.0), axis=1, keepdims=True)
        slot = routes_ref[:, j : j + 1] * (slots // experts) + rank.astype(jnp.int32)
        pick = jnp.where(slot_lanes == slot, 1.0, 0.0)
        ref[...] = pick.astype(BF16)
        picks.append(pick)

    def store(expert, blocks):
        chips = blocks.shape[0] // 4
        held_ref[expert // 4 : expert // 4 + chips] = blocks.reshape(chips, 2, 2, 8, width)

    slot_rows((picks[0] + picks[1]).astype(BF16), cot_ref[...], 128, store)
    for other in range(2):
        at = 3 * WIDE + width * other
        which = mine_ref[0] if other == 0 else 1 - mine_ref[0]
        copies.append(
            pltpu.make_async_copy(
                held_ref.at[:, :, which], out_ref.at[:, :, :, at : at + width], sems.at[6 + other]
            )
        )
        copies[-1].start()
    for copy in copies:
        copy.wait()


def attend_body(head_width, off_ref, qkv_ref, out_ref):
    frames = qkv_ref.shape[0]
    q, k, v = [
        rows_of(qkv_ref[:, :, WIDE * s : WIDE * s + WIDE]).astype(BF16) for s in range(3)
    ]
    rows = frames * 8
    off = off_ref[0]
    same = (
        lax.broadcasted_iota(jnp.int32, (rows, rows), 0) & 7
    ) == (lax.broadcasted_iota(jnp.int32, (rows, rows), 1) & 7)
    lane = lax.broadcasted_iota(jnp.int32, (rows, 256), 1)
    tiles = [jnp.zeros((rows, 128), F32) for _ in range(WIDE // 128)]
    for h in range(H // 2):
        w = h // 2
        first = off + head_width * h - 128 * w
        inside = (lane >= first) & (lane < first + head_width)
        cols = slice(128 * w, 128 * w + 256)
        mine = jnp.where(inside, q[:, cols].astype(F32), 0.0).astype(BF16)
        scores = lax.dot_general(
            mine, k[:, cols], (((1,), (1,)), ((), ())), preferred_element_type=F32
        ) * head_width ** (-0.5)
        scores = jnp.where(same, scores, -1e30)
        peak = jnp.max(scores, axis=1, keepdims=True)
        weights = jnp.exp(scores - peak)
        probs = (weights / jnp.sum(weights, axis=1, keepdims=True)).astype(BF16)
        got = jnp.dot(probs, v[:, cols], preferred_element_type=F32)
        for t in range(2):
            part = slice(128 * t, 128 * t + 128)
            tiles[w + t] = jnp.where(inside[:, part], got[:, part], tiles[w + t])
    for t, tile in enumerate(tiles):
        out_ref[:, :, 128 * t : 128 * t + 128] = blocks_of(tile)


def inv_rms_of(hidden_float):
    return lax.rsqrt(jnp.mean(hidden_float * hidden_float, axis=-1, keepdims=True) + 1e-06)


def project_body(
    att_ref, residual_ref, w_out_ref, gain_ref, w_router_ref, routes_ref, pick0_ref, pick1_ref,
    hidden_ref, combine_ref, out_ref,
):
    low, high = rows_of(att_ref[:, 0]), rows_of(att_ref[:, 1])
    shared = WIDE - STEP
    attended = jnp.concatenate(
        [low[:, :STEP], low[:, STEP:] + high[:, :shared], high[:, shared:]], axis=1
    ).astype(BF16)
    stream = residual_ref[...].astype(F32) + jnp.dot(
        attended, w_out_ref[...], preferred_element_type=F32
    )
    hidden = stream.astype(BF16)
    hidden_ref[...] = hidden
    hidden_float = hidden.astype(F32)
    normed = (hidden_float * inv_rms_of(hidden_float) * gain_ref[...]).astype(BF16)

    def store(expert, blocks):
        for half in range(2):
            out_ref[expert : expert + blocks.shape[0], half] = blocks

    slot_rows(pick0_ref[...] + pick1_ref[...], normed, 128, store)
    logits = jnp.dot(normed, w_router_ref[...], preferred_element_type=F32)
    onehots = pair_onehots(routes_ref, w_router_ref.shape[1])
    for j in range(2):
        chosen = jnp.sum(jnp.where(onehots[j], logits, 0.0), axis=1, keepdims=True)
        combine_ref[:, j : j + 1] = jax.nn.sigmoid(chosen)


def expert_body(
    place_ref, x_ref, cot0_ref, cot1_ref, cot2_ref, cot3_ref, w_router_ref, gate_ref, up_ref,
    down_ref, out_ref, scaled_ref, units_ref, d_gate_ref, d_up_ref, cot_ref,
):
    turned = (((1,), (1,)), ((), ()))
    for n, ref in enumerate((cot0_ref, cot1_ref, cot2_ref, cot3_ref)):
        cot_ref[:, place_ref[1 + n]] = ref[...]
    frames, planes, eight, width = cot_ref.shape
    x = x_ref[...]
    pre_gate = jnp.dot(x, gate_ref[...], preferred_element_type=F32)
    pre_up = jnp.dot(x, up_ref[...], preferred_element_type=F32)
    gate_sig = jax.nn.sigmoid(pre_gate)
    gate_act = pre_gate * gate_sig
    units = (gate_act * pre_up).astype(BF16)
    units_ref[...] = units
    out_ref[:, :eight] = blocks_of(jnp.dot(units, down_ref[...], preferred_element_type=F32))
    logits = jnp.dot(x, w_router_ref[...], preferred_element_type=F32)
    lanes = lax.broadcasted_iota(jnp.int32, logits.shape, 1)
    chosen = jnp.sum(jnp.where(lanes == place_ref[0], logits, 0.0), axis=1, keepdims=True)
    cotangent = rows_of(cot_ref[...].reshape(frames * planes, eight, width))
    scaled = (jax.nn.sigmoid(chosen) * cotangent).astype(BF16)
    scaled_ref[...] = scaled
    d_units = lax.dot_general(scaled, down_ref[...], turned, preferred_element_type=F32)
    slope = pre_up * (gate_sig + gate_act * (1.0 - gate_sig))
    d_pre_gate = (d_units * slope).astype(BF16)
    d_pre_up = (d_units * gate_act).astype(BF16)
    d_gate_ref[...] = d_pre_gate
    d_up_ref[...] = d_pre_up
    out_ref[:, eight:] = blocks_of(
        lax.dot_general(d_pre_gate, gate_ref[...], turned, preferred_element_type=F32)
        + lax.dot_general(d_pre_up, up_ref[...], turned, preferred_element_type=F32)
    )


def pair_sum(ref, rows):
    return (rows_of(ref[:, 0, rows]) + rows_of(ref[:, 1, rows])).astype(BF16)


def finish_body(
    back_ref, pick0_ref, pick1_ref, combine_ref, cot_ref, hidden_ref, gain_ref, w_router_ref,
    routes_ref, block_ref, d_hidden_ref, got_ref,
):
    step = pl.program_id(0)
    outs = pair_sum(back_ref, slice(0, 8))
    ins = pair_sum(back_ref, slice(8, 16))
    picks = [pick0_ref[...], pick1_ref[...]]
    new = [
        jnp.dot(picks[0], outs, preferred_element_type=F32),
        jnp.dot(picks[1], outs, preferred_element_type=F32),
        jnp.dot(picks[0] + picks[1], ins, preferred_element_type=F32),
    ]

    @pl.when(step == 0)
    def _():
        for n in range(3):
            got_ref[n] = new[n]

    @pl.when(step > 0)
    def _():
        for n in range(3):
            got_ref[n] = got_ref[n] + new[n]

    @pl.when(step == pl.num_programs(0) - 1)
    def _():
        cotangent = cot_ref[...].astype(F32)
        hidden_float = hidden_ref[...].astype(F32)
        block = hidden_float
        onehots = pair_onehots(routes_ref, w_router_ref.shape[1])
        rows = jnp.zeros(onehots[0].shape, F32)
        for j in range(2):
            combine = combine_ref[:, j : j + 1]
            expert_out = got_ref[j]
            block = block + combine * expert_out
            d_combine = jnp.sum(cotangent * expert_out, axis=1, keepdims=True)
            rows = rows + jnp.where(onehots[j], d_combine * combine * (1.0 - combine), 0.0)
        block_ref[...] = block.astype(BF16)
        d_normed = got_ref[2] + lax.dot_general(
            rows,
            w_router_ref[...].astype(F32),
            (((1,), (1,)), ((), ())),
            precision=lax.Precision.HIGHEST,
            preferred_element_type=F32,
        )
        inv_rms = inv_rms_of(hidden_float)
        gained = d_normed * gain_ref[...]
        d_norm_in = inv_rms * gained - hidden_float * inv_rms**3 * jnp.mean(
            gained * hidden_float, axis=-1, keepdims=True
        )
        d_hidden_ref[...] = (cotangent + d_norm_in).astype(BF16)


def relay(parcel, axes):
    return lax.all_to_all(parcel, axes, split_axis=0, concat_axis=0, tiled=True)


def on_device(
    residual, queries, keys_in, values, w_out, norm_gain, w_router, routes, w_gate, w_up, w_down,
    d_out,
):
    everyone = ("frames", "expert")
    frames = lax.axis_size("frames")
    devices = frames * lax.axis_size("expert")
    width = residual.shape[2]
    tok = residual.shape[0] * residual.shape[1]
    experts = w_router.shape[1]
    cap = 4 * tok // experts
    slots = experts * cap
    hidden_units = w_gate.shape[2]
    smem = pl.BlockSpec(memory_space=pltpu.SMEM)
    vmem = pl.BlockSpec(memory_space=pltpu.VMEM)
    anywhere = pl.BlockSpec(memory_space=pl.ANY)
    flat = lambda a: a.reshape(tok, width)
    eights = lambda a: a.reshape(tok // 8, 8, width)
    cot = flat(d_out)
    picked = routes.reshape(tok, 2)
    gain = norm_gain.reshape(1, width)
    me, plane = lax.axis_index("frames"), lax.axis_index("expert")
    offset = (me % 2 * (width // 2 - STEP)).reshape(1)

    full = 3 * WIDE + 2 * width
    packed, pick0, pick1 = call(
        lambda *refs: pack_body(experts, *refs),
        (shape((frames // 2, 2, 8, full), BF16), shape((tok, slots), BF16),
         shape((tok, slots), BF16)),
        (2 * tok * slots * width, 2 * frames * 8 * full * 2),
        in_specs=[smem, vmem, vmem, anywhere, anywhere, anywhere],
        out_specs=(anywhere, vmem, vmem),
        scratch_shapes=[
            pltpu.VMEM((frames // 2, 2, 2, 8, width), BF16),
            pltpu.SemaphoreType.DMA((8,)),
        ],
    )((plane // 2).reshape(1), picked, cot, eights(queries), eights(keys_in), eights(values))
    mixed = relay(packed.reshape(frames, 8, full), "frames")
    attended = call(
        lambda *refs: attend_body(width // H, *refs),
        shape((frames, 8, WIDE), BF16),
        (1 << 29, 4 * frames * 8 * WIDE * 2),
        grid=(1,),
        in_specs=[smem, pl.BlockSpec((frames, 8, 3 * WIDE), lambda i: (0, 0, 0))],
        out_specs=pl.BlockSpec((frames, 8, WIDE), lambda i: (0, 0, 0)),
    )(offset, mixed)
    attended = relay(attended, "frames").reshape(frames // 2, 2, 8, WIDE)
    near = [(0, 1), (1, 0), (2, 3), (3, 2)]
    far = [(0, 3), (3, 0), (1, 2), (2, 1)]
    cots = [mixed[:, :, 3 * WIDE : 3 * WIDE + width]]
    cots.append(lax.ppermute(cots[0], "expert", near))
    cots.append(lax.ppermute(mixed[:, :, 3 * WIDE + width :], "expert", far))
    cots.append(lax.ppermute(cots[2], "expert", near))
    hidden, combine, outbound = call(
        project_body,
        (shape((tok, width), BF16), shape((tok, 2), F32), shape((experts, 2, cap, width), BF16)),
        (2 * tok * width * (width + slots), (width + 3 * slots) * width * 2),
    )(attended, flat(residual), w_out, gain, w_router, picked, pick0, pick1)
    arrived = relay(outbound.reshape(devices, cap, width), everyone)

    total = devices * cap
    block = 256
    by_rows = lambda w: pl.BlockSpec((block, w), lambda i: (i, 0))
    by_blocks = lambda n, m: pl.BlockSpec((n, m, width), lambda i: (i, 0, 0))
    whole = lambda a: pl.BlockSpec(a.shape, lambda i: (0, 0))
    gate_w, up_w, down_w = w_gate[0], w_up[0], w_down[0]
    x = arrived.reshape(total, width)
    product = 2 * total * width * hidden_units
    place = jnp.stack(
        [(me * 4 + plane) // 2, plane, plane ^ 1, 3 - plane, (3 - plane) ^ 1]
    ).astype(jnp.int32)
    per = block // 32
    returned, scaled, units, d_pre_gate, d_pre_up = call(
        expert_body,
        (
            shape((devices, 2 * cap, width), BF16),
            shape((total, width), BF16),
            shape((total, hidden_units), BF16),
            shape((total, hidden_units), BF16),
            shape((total, hidden_units), BF16),
        ),
        (6 * product, 10 * total * width * 2),
        grid=(total // block,),
        in_specs=[smem, by_rows(width)] + [by_blocks(per, 8)] * 4
        + [whole(w_router), whole(gate_w), whole(up_w), whole(down_w)],
        out_specs=[by_blocks(block // 8, 2 * cap), by_rows(width)] + [by_rows(hidden_units)] * 3,
        scratch_shapes=[pltpu.VMEM((per, 4, 8, width), BF16)],
    )(place, x, *cots, w_router, gate_w, up_w, down_w)
    back = relay(returned, everyone).reshape(experts, 2, 2 * cap, width)
    d_down = jnp.dot(units.T, scaled, preferred_element_type=F32)
    d_gate = jnp.dot(x.T, d_pre_gate, preferred_element_type=F32)
    d_up = jnp.dot(x.T, d_pre_up, preferred_element_type=F32)

    part = experts // 4
    by_slots = pl.BlockSpec((tok, part * cap), lambda i: (0, i))
    block_out, d_hidden = call(
        finish_body,
        (shape((tok, width), BF16), shape((tok, width), BF16)),
        (6 * tok * width * slots, 4 * slots * width * 2),
        grid=(4,),
        in_specs=[
            pl.BlockSpec((part, 2, 2 * cap, width), lambda i: (i, 0, 0, 0)), by_slots, by_slots,
            whole(combine), whole(cot), whole(hidden), whole(gain), whole(w_router),
            whole(picked),
        ],
        out_specs=(whole(cot), whole(cot)),
        scratch_shapes=[pltpu.VMEM((3, tok, width), F32)],
    )(back, pick0, pick1, combine, cot, hidden, gain, w_router, picked)
    return (
        block_out.reshape(residual.shape),
        d_hidden.reshape(residual.shape),
        d_gate[None],
        d_up[None],
        d_down[None],
    )


def solution(mesh):
    tokens = P("frames", "expert", None)
    weights = P(("frames", "expert"), None, None)
    return jax.shard_map(
        on_device,
        mesh=mesh,
        in_specs=(tokens,) * 4
        + (P(), P(), P(), P("expert", "frames", None, None))
        + (weights,) * 3
        + (tokens,),
        out_specs=(tokens, tokens, weights, weights, weights),
        check_vma=False,
    )
```

```python
import functools

import jax
import jax.numpy as jnp
from jax import lax
from jax.experimental import pallas as pl
from jax.experimental.pallas import tpu as pltpu
from jax.sharding import PartitionSpec as P

H = 16
F32 = jnp.float32
BF16 = jnp.bfloat16
WIDE = 640
STEP = 512
ROOMY = 60 * 1024 * 1024
SNUG = 32 * 1024 * 1024


def call(body, outs, cost, limit=SNUG, **extra):
    flops, moved = cost
    return pl.pallas_call(
        body,
        out_shape=outs,
        compiler_params=pltpu.CompilerParams(vmem_limit_bytes=limit),
        cost_estimate=pl.CostEstimate(flops=flops, bytes_accessed=moved, transcendentals=0),
        **extra,
    )


def shape(dims, dtype):
    return jax.ShapeDtypeStruct(dims, dtype)


def rows_of(blocks):
    n, eight, width = blocks.shape
    return blocks.astype(F32).reshape(n * eight, width)


def blocks_of(rows):
    total, width = rows.shape
    return rows.reshape(total // 8, 8, width).astype(BF16)


def pack_body(q_ref, k_ref, v_ref, out_ref):
    for s, ref in enumerate((q_ref, k_ref, v_ref)):
        for i in range(ref.shape[0]):
            for half in range(2):
                out_ref[i, half, 8 * s : 8 * s + 8, :] = ref[
                    i, :, STEP * half : STEP * half + WIDE
                ]


def iota(dims, axis):
    return lax.broadcasted_iota(jnp.int32, dims, axis)


def slot_lines(routes_ref, experts, cap):
    tok = routes_ref.shape[1]
    lines = [routes_ref[j : j + 1, :] for j in range(2)]
    onehots = [iota((experts, tok), 0) == line for line in lines]
    named = jnp.where(onehots[0] | onehots[1], 1.0, 0.0).astype(BF16)
    later = jnp.where(iota((tok, tok), 0) < iota((tok, tok), 1), 1.0, 0.0).astype(BF16)
    before = jnp.dot(named, later, preferred_element_type=F32)
    found = []
    for line, onehot in zip(lines, onehots):
        rank = jnp.sum(jnp.where(onehot, before, 0.0), axis=0, keepdims=True)
        place = (line & -4) | ((line & 1) << 1) | ((line >> 1) & 1)
        found.append((line.astype(F32), place.astype(F32) * cap + rank))
    return found


def slot_onehots(lines, slots):
    where = iota((slots, lines[0][1].shape[1]), 0).astype(F32)
    return [jnp.where(where == slot, 1.0, 0.0).astype(BF16) for _, slot in lines]


def expert_onehots(lines, experts):
    tok = lines[0][0].shape[1]
    diagonal = iota((tok, tok), 0) == iota((tok, tok), 1)
    found = []
    for expert, _ in lines:
        column = jnp.sum(jnp.where(diagonal, expert, 0.0), axis=1, keepdims=True)
        found.append(iota((tok, experts), 1) == column.astype(jnp.int32))
    return found


def attend_body(head_width, off_ref, qkv_ref, out_ref):
    frames = qkv_ref.shape[0]
    q, k, v = [rows_of(qkv_ref[:, 8 * s : 8 * s + 8, :]).astype(BF16) for s in range(3)]
    rows = frames * 8
    off = off_ref[0]
    same = (
        lax.broadcasted_iota(jnp.int32, (rows, rows), 0) & 7
    ) == (lax.broadcasted_iota(jnp.int32, (rows, rows), 1) & 7)
    lane = lax.broadcasted_iota(jnp.int32, (rows, 256), 1)
    tiles = [jnp.zeros((rows, 128), F32) for _ in range(WIDE // 128)]
    for h in range(H // 2):
        w = h // 2
        first = off + head_width * h - 128 * w
        inside = (lane >= first) & (lane < first + head_width)
        cols = slice(128 * w, 128 * w + 256)
        mine = jnp.where(inside, q[:, cols].astype(F32), 0.0).astype(BF16)
        scores = lax.dot_general(
            mine, k[:, cols], (((1,), (1,)), ((), ())), preferred_element_type=F32
        ) * head_width ** (-0.5)
        scores = jnp.where(same, scores, -1e30)
        peak = jnp.max(scores, axis=1, keepdims=True)
        weights = jnp.exp(scores - peak)
        probs = (weights / jnp.sum(weights, axis=1, keepdims=True)).astype(BF16)
        got = jnp.dot(probs, v[:, cols], preferred_element_type=F32)
        for t in range(2):
            part = slice(128 * t, 128 * t + 128)
            tiles[w + t] = jnp.where(inside[:, part], got[:, part], tiles[w + t])
    for t, tile in enumerate(tiles):
        out_ref[:, :, 128 * t : 128 * t + 128] = blocks_of(tile)


def inv_rms_of(hidden_float):
    return lax.rsqrt(jnp.mean(hidden_float * hidden_float, axis=-1, keepdims=True) + 1e-06)


def project_body(
    att_ref, residual_ref, w_out_ref, gain_ref, w_router_ref, routes_ref, cot_ref,
    hidden_ref, combine_ref, out_ref,
):
    low, high = rows_of(att_ref[:, 0]), rows_of(att_ref[:, 1])
    shared = WIDE - STEP
    attended = jnp.concatenate(
        [low[:, :STEP], low[:, STEP:] + high[:, :shared], high[:, shared:]], axis=1
    ).astype(BF16)
    stream = residual_ref[...].astype(F32) + jnp.dot(
        attended, w_out_ref[...], preferred_element_type=F32
    )
    hidden = stream.astype(BF16)
    hidden_ref[...] = hidden
    hidden_float = hidden.astype(F32)
    normed = (hidden_float * inv_rms_of(hidden_float) * gain_ref[...]).astype(BF16)
    chips, _, planes, cap, width = out_ref.shape
    experts = chips * planes
    lines = slot_lines(routes_ref, experts, cap)
    picks = slot_onehots(lines, experts * cap)
    picks = picks[0] + picks[1]
    step = 4
    for core, rows in enumerate((normed, cot_ref[...])):
        for at in range(0, chips, step):
            some = picks[at * planes * cap : (at + step) * planes * cap]
            blocks = blocks_of(jnp.dot(some, rows, preferred_element_type=F32))
            out_ref[at : at + step, core] = blocks.reshape(step, planes, cap, width)
    logits = jnp.dot(normed, w_router_ref[...], preferred_element_type=F32)
    for j, onehot in enumerate(expert_onehots(lines, experts)):
        chosen = jnp.sum(jnp.where(onehot, logits, 0.0), axis=1, keepdims=True)
        combine_ref[:, j : j + 1] = jax.nn.sigmoid(chosen)


def expert_body(
    state_ref, here_ref, there_ref, column_ref,
    home_gate_ref, home_up_ref, home_down_ref, new_gate_ref, new_up_ref, new_down_ref,
    keep_ref, send_ref, scaled_ref, units_ref, d_gate_ref, d_up_ref,
    gate_ref, up_ref, down_ref, sems,
):
    turned = (((1,), (1,)), ((), ()))
    first, moved = state_ref[0] == 0, state_ref[1] == 1
    opening = pl.program_id(0) == 0
    targets = (gate_ref, up_ref, down_ref)

    def fetch(sources):
        for n, (source, target) in enumerate(zip(sources, targets)):
            pltpu.make_async_copy(source, target, sems.at[n]).start()

    @pl.when(opening & moved)
    def _():
        fetch((new_gate_ref, new_up_ref, new_down_ref))

    @pl.when(opening & jnp.logical_not(moved))
    def _():
        fetch((home_gate_ref, home_up_ref, home_down_ref))

    def arrived(n):
        @pl.when(opening)
        def _():
            pltpu.make_async_copy(home_gate_ref if n < 2 else home_down_ref, targets[n],
                                  sems.at[n]).wait()

    def work(rows_ref, cot_ref, out_ref, in_ref):
        x = rows_ref[...]
        arrived(0)
        pre_gate = jnp.dot(x, gate_ref[0], preferred_element_type=F32)
        arrived(1)
        pre_up = jnp.dot(x, up_ref[0], preferred_element_type=F32)
        gate_sig = jax.nn.sigmoid(pre_gate)
        gate_act = pre_gate * gate_sig
        units = (gate_act * pre_up).astype(BF16)
        units_ref[...] = units
        arrived(2)
        out_ref[...] = jnp.dot(units, down_ref[0], preferred_element_type=F32).astype(BF16)
        chosen = jnp.sum(x.astype(F32) * column_ref[...], axis=1, keepdims=True)
        scaled = (jax.nn.sigmoid(chosen) * cot_ref[...].astype(F32)).astype(BF16)
        scaled_ref[...] = scaled
        d_units = lax.dot_general(scaled, down_ref[0], turned, preferred_element_type=F32)
        slope = pre_up * (gate_sig + gate_act * (1.0 - gate_sig))
        d_pre_gate = (d_units * slope).astype(BF16)
        d_pre_up = (d_units * gate_act).astype(BF16)
        d_gate_ref[...] = d_pre_gate
        d_up_ref[...] = d_pre_up
        in_ref[...] = (
            lax.dot_general(d_pre_gate, gate_ref[0], turned, preferred_element_type=F32)
            + lax.dot_general(d_pre_up, up_ref[0], turned, preferred_element_type=F32)
        ).astype(BF16)

    @pl.when(first)
    def _():
        work(here_ref, there_ref, keep_ref, send_ref)

    @pl.when(jnp.logical_not(first))
    def _():
        work(there_ref, here_ref, send_ref, keep_ref)


def down_body(units_ref, scaled_ref, out_ref):
    out_ref[0] = lax.dot_general(
        units_ref[...], scaled_ref[...], (((0,), (0,)), ((), ())), preferred_element_type=F32
    ).astype(BF16)


def gates_body(state_ref, here_ref, there_ref, left_ref, right_ref, gate_ref, up_ref):
    def work(x_ref):
        for ref, out_ref in ((left_ref, gate_ref), (right_ref, up_ref)):
            out_ref[0] = lax.dot_general(
                x_ref[...], ref[...], (((0,), (0,)), ((), ())), preferred_element_type=F32
            ).astype(BF16)

    for core, x_ref in enumerate((here_ref, there_ref)):
        pl.when(state_ref[0] == core)(functools.partial(work, x_ref))


def widen_body(state_ref, home_ref, new_ref, out_ref):
    out_ref[...] = jnp.where(state_ref[1] == 1, new_ref[...], home_ref[...]).astype(F32)


def spread(onehot, rows):
    return lax.dot_general(onehot, rows, (((0,), (0,)), ((), ())), preferred_element_type=F32)


def finish_body(
    back_ref, routes_ref, combine_ref, cot_ref, hidden_ref, gain_ref, w_router_ref,
    block_ref, d_hidden_ref, got_ref,
):
    chips, _, planes, cap, width = back_ref.shape
    experts = chips * planes
    tok = hidden_ref.shape[0]
    lines = slot_lines(routes_ref, experts, cap)
    picks = slot_onehots(lines, experts * cap)
    either = picks[0] + picks[1]
    combines = [combine_ref[:, j : j + 1] for j in range(2)]
    d_combines = [jnp.zeros((tok, 1), F32) for _ in range(2)]
    for at in range(0, width, 384):
        cols = slice(at, at + 384)
        outs, ins = [
            rows_of(back_ref[:, core, :, :, cols].reshape(experts, cap, 384)).astype(BF16)
            for core in range(2)
        ]
        got_ref[:, cols] = spread(either, ins)
        cotangent = cot_ref[:, cols].astype(F32)
        block = hidden_ref[:, cols].astype(F32)
        for j in range(2):
            expert_out = spread(picks[j], outs)
            block = block + combines[j] * expert_out
            d_combines[j] = d_combines[j] + jnp.sum(
                cotangent * expert_out, axis=1, keepdims=True
            )
        block_ref[:, cols] = block.astype(BF16)
    rows = jnp.zeros((tok, experts), F32)
    for j, onehot in enumerate(expert_onehots(lines, experts)):
        d_logit = d_combines[j] * combines[j] * (1.0 - combines[j])
        rows = rows + jnp.where(onehot, d_logit, 0.0)
    d_normed = got_ref[...] + lax.dot_general(
        rows,
        w_router_ref[...].astype(F32),
        (((1,), (1,)), ((), ())),
        precision=lax.Precision.HIGHEST,
        preferred_element_type=F32,
    )
    hidden_float = hidden_ref[...].astype(F32)
    inv_rms = inv_rms_of(hidden_float)
    gained = d_normed * gain_ref[...]
    d_norm_in = inv_rms * gained - hidden_float * inv_rms**3 * jnp.mean(
        gained * hidden_float, axis=-1, keepdims=True
    )
    d_hidden_ref[...] = (cot_ref[...].astype(F32) + d_norm_in).astype(BF16)


def relay(parcel, axes):
    return lax.all_to_all(parcel, axes, split_axis=0, concat_axis=0, tiled=True)


def on_device(
    residual, queries, keys_in, values, w_out, norm_gain, w_router, routes, w_gate, w_up, w_down,
    d_out,
):
    everyone = ("frames", "expert")
    frames = lax.axis_size("frames")
    planes = lax.axis_size("expert")
    devices = frames * planes
    chips = frames // 2
    width = residual.shape[2]
    tok = residual.shape[0] * residual.shape[1]
    experts = w_router.shape[1]
    cap = 4 * tok // experts
    slots = experts * cap
    hidden_units = w_gate.shape[2]
    smem = pl.BlockSpec(memory_space=pltpu.SMEM)
    fixed = lambda *dims: pl.BlockSpec(dims, lambda i: (0,) * len(dims))
    whole = lambda a: fixed(*a.shape)
    flat = lambda a: a.reshape(tok, width)
    eights = lambda a: a.reshape(tok // 8, 8, width)
    cot = flat(d_out)
    pairs = jnp.swapaxes(routes.reshape(tok, 2), 0, 1)
    gain = norm_gain.reshape(1, width)
    me, plane = lax.axis_index("frames"), lax.axis_index("expert")
    core = me % 2
    offset = (core * (width // 2 - STEP)).reshape(1)
    mine = 4 * (me // 2) + 2 * (plane % 2) + plane // 2
    column = lax.dynamic_slice(w_router, (0, mine), (width, 1)).astype(F32).reshape(1, width)
    swaps = [
        (f * planes + z, (f ^ 1) * planes + (z ^ 1))
        for f in range(frames)
        for z in range(planes)
        if (f + z) % 2
    ]
    state = jnp.stack([core, (me + plane) % 2]).astype(jnp.int32)
    swap = lambda a: lax.ppermute(a, everyone, swaps)
    beside = lambda a: lax.ppermute(a, "frames", [(i, i ^ 1) for i in range(frames)])

    moved_w = [swap(w) for w in (w_gate, w_up, w_down)]
    part = tok // 32
    packed = call(
        pack_body,
        shape((chips, 2, 24, WIDE), BF16),
        (0, 2 * frames * 24 * WIDE * 2),
        limit=ROOMY,
        grid=(4,),
        in_specs=[pl.BlockSpec((part, 8, width), lambda i: (i, 0, 0))] * 3,
        out_specs=pl.BlockSpec((part, 2, 24, WIDE), lambda i: (i, 0, 0, 0)),
    )(eights(queries), eights(keys_in), eights(values))
    qkv = relay(packed.reshape(frames, 24, WIDE), "frames")
    attended = call(
        lambda *refs: attend_body(width // H, *refs),
        shape((frames, 8, WIDE), BF16),
        (1 << 29, 4 * frames * 8 * WIDE * 2),
        grid=(1,),
        in_specs=[smem, fixed(frames, 24, WIDE)],
        out_specs=fixed(frames, 8, WIDE),
    )(offset, qkv)
    attended = relay(attended, "frames").reshape(chips, 2, 8, WIDE)
    hidden, combine, outbound = call(
        project_body,
        (shape((tok, width), BF16), shape((tok, 2), F32),
         shape((chips, 2, planes, cap, width), BF16)),
        (2 * tok * width * (width + 2 * slots), (width + 3 * slots) * width * 2),
        grid=(1,),
        in_specs=[whole(attended), whole(cot), whole(w_out), whole(gain), whole(w_router),
                  whole(pairs), whole(cot)],
        out_specs=(whole(cot), fixed(tok, 2), fixed(chips, 2, planes, cap, width)),
    )(attended, flat(residual), w_out, gain, w_router, pairs, cot)
    outbound, *moved_w = lax.optimization_barrier((outbound, *moved_w))
    here = relay(outbound.reshape(devices, cap, width), everyone)
    there = beside(here)

    total = devices * cap
    block = 512
    by_rows = lambda w: pl.BlockSpec((block, w), lambda i: (i, 0))
    rows = lambda a: a.reshape(total, width)
    product = 2 * total * width * hidden_units
    wide = shape((total, width), BF16)
    inner = shape((total, hidden_units), BF16)
    hbm = pl.BlockSpec(memory_space=pltpu.HBM)
    keep, send, scaled, units, d_pre_gate, d_pre_up = call(
        expert_body,
        (wide, wide, wide, inner, inner, inner),
        (6 * product, 10 * total * width * 2),
        limit=ROOMY,
        grid=(total // block,),
        in_specs=[smem, by_rows(width), by_rows(width), whole(column)] + [hbm] * 6,
        out_specs=[by_rows(width)] * 3 + [by_rows(hidden_units)] * 3,
        scratch_shapes=[
            pltpu.VMEM(w_gate.shape, BF16),
            pltpu.VMEM(w_up.shape, BF16),
            pltpu.VMEM(w_down.shape, BF16),
            pltpu.SemaphoreType.DMA((3,)),
        ],
    )(state, rows(here), rows(there), column, w_gate, w_up, w_down, *moved_w)
    got = beside(send)
    third = width // 3
    by_third = pl.BlockSpec((total, third), lambda i: (0, i))
    d_down = call(
        down_body,
        shape(w_down.shape, BF16),
        (product, 2 * total * width * 2),
        limit=ROOMY,
        grid=(3,),
        in_specs=[whole(units), by_third],
        out_specs=pl.BlockSpec((1, hidden_units, third), lambda i: (0, 0, i)),
    )(units, scaled)
    got, d_down = lax.optimization_barrier((got, d_down))
    returned = (keep.astype(F32) + got.astype(F32)).astype(BF16)
    back = relay(returned.reshape(devices, cap, width), everyone)
    back = back.reshape(chips, 2, planes, cap, width)

    def chosen(core_index):
        return lambda i, state: (0, jnp.where(state[0] == core_index, i, 0))

    still = lambda i, state: (0, 0)
    d_gate, d_up = pl.pallas_call(
        gates_body,
        out_shape=(shape(w_gate.shape, BF16), shape(w_up.shape, BF16)),
        grid_spec=pltpu.PrefetchScalarGridSpec(
            num_scalar_prefetch=1,
            grid=(3,),
            in_specs=[
                pl.BlockSpec((total, third), chosen(0)),
                pl.BlockSpec((total, third), chosen(1)),
                pl.BlockSpec((total, hidden_units), still),
                pl.BlockSpec((total, hidden_units), still),
            ],
            out_specs=[pl.BlockSpec((1, third, hidden_units), lambda i, state: (0, i, 0))] * 2,
        ),
        compiler_params=pltpu.CompilerParams(vmem_limit_bytes=ROOMY),
        cost_estimate=pl.CostEstimate(
            flops=2 * product, bytes_accessed=4 * total * width * 2, transcendentals=0
        ),
    )(state, rows(here), rows(there), d_pre_gate, d_pre_up)

    def widen(home, new):
        _, height, across = home.shape
        part = height // 4
        pick = lambda n: lambda i, state: (0, jnp.where(state[1] == n, i, 0), 0)
        return pl.pallas_call(
            widen_body,
            out_shape=shape(home.shape, F32),
            grid_spec=pltpu.PrefetchScalarGridSpec(
                num_scalar_prefetch=1,
                grid=(4,),
                in_specs=[pl.BlockSpec((1, part, across), pick(n)) for n in range(2)],
                out_specs=pl.BlockSpec((1, part, across), lambda i, state: (0, i, 0)),
            ),
            compiler_params=pltpu.CompilerParams(vmem_limit_bytes=SNUG),
            cost_estimate=pl.CostEstimate(
                flops=height * across, bytes_accessed=6 * height * across, transcendentals=0
            ),
        )(state, home, new)

    new_down = swap(d_down)
    new_gate = swap(d_gate)
    d_up, new_down = lax.optimization_barrier((d_up, new_down))
    new_up = swap(d_up)
    block_out, d_hidden = call(
        finish_body,
        (shape((tok, width), BF16), shape((tok, width), BF16)),
        (6 * tok * width * slots, 4 * slots * width * 2),
        limit=ROOMY,
        grid=(1,),
        in_specs=[whole(back), whole(pairs), whole(combine), whole(cot), whole(hidden),
                  whole(gain), whole(w_router)],
        out_specs=(whole(cot), whole(cot)),
        scratch_shapes=[pltpu.VMEM((tok, width), F32)],
    )(back, pairs, combine, cot, hidden, gain, w_router)
    new_up, d_hidden = lax.optimization_barrier((new_up, d_hidden))
    d_down, d_gate, d_up = [
        widen(*pair) for pair in ((d_down, new_down), (d_gate, new_gate), (d_up, new_up))
    ]
    return (
        block_out.reshape(residual.shape),
        d_hidden.reshape(residual.shape),
        d_gate,
        d_up,
        d_down,
    )


def solution(mesh):
    tokens = P("frames", "expert", None)
    weights = P(("frames", "expert"), None, None)
    return jax.shard_map(
        on_device,
        mesh=mesh,
        in_specs=(tokens,) * 4
        + (P(), P(), P(), P("expert", "frames", None, None))
        + (weights,) * 3
        + (tokens,),
        out_specs=(tokens, tokens, weights, weights, weights),
        check_vma=False,
    )
```

```python
import functools

import jax
import jax.numpy as jnp
from jax import lax
from jax.experimental import pallas as pl
from jax.experimental.pallas import tpu as pltpu
from jax.sharding import PartitionSpec as P

H = 16
F32 = jnp.float32
BF16 = jnp.bfloat16
WIDE = 640
STEP = 512
ROOMY = 60 * 1024 * 1024
SNUG = 32 * 1024 * 1024


def call(body, outs, cost, limit=SNUG, **extra):
    flops, moved = cost
    return pl.pallas_call(
        body,
        out_shape=outs,
        compiler_params=pltpu.CompilerParams(vmem_limit_bytes=limit),
        cost_estimate=pl.CostEstimate(flops=flops, bytes_accessed=moved, transcendentals=0),
        **extra,
    )


def shape(dims, dtype):
    return jax.ShapeDtypeStruct(dims, dtype)


def rows_of(blocks):
    n, eight, width = blocks.shape
    return blocks.astype(F32).reshape(n * eight, width)


def blocks_of(rows):
    total, width = rows.shape
    return rows.reshape(total // 8, 8, width).astype(BF16)


def pack_body(q_ref, k_ref, v_ref, out_ref):
    for s, ref in enumerate((q_ref, k_ref, v_ref)):
        for i in range(ref.shape[0]):
            for half in range(2):
                out_ref[i, half, 8 * s : 8 * s + 8, :] = ref[
                    i, :, STEP * half : STEP * half + WIDE
                ]


def iota(dims, axis):
    return lax.broadcasted_iota(jnp.int32, dims, axis)


def slot_lines(routes_ref, experts, cap):
    tok = routes_ref.shape[1]
    lines = [routes_ref[j : j + 1, :] for j in range(2)]
    onehots = [iota((experts, tok), 0) == line for line in lines]
    named = jnp.where(onehots[0] | onehots[1], 1.0, 0.0).astype(BF16)
    later = jnp.where(iota((tok, tok), 0) < iota((tok, tok), 1), 1.0, 0.0).astype(BF16)
    before = jnp.dot(named, later, preferred_element_type=F32)
    found = []
    for line, onehot in zip(lines, onehots):
        rank = jnp.sum(jnp.where(onehot, before, 0.0), axis=0, keepdims=True)
        place = (line & -4) | ((line & 1) << 1) | ((line >> 1) & 1)
        found.append((line.astype(F32), place.astype(F32) * cap + rank))
    return found


def slot_onehots(lines, slots):
    where = iota((slots, lines[0][1].shape[1]), 0).astype(F32)
    return [jnp.where(where == slot, 1.0, 0.0).astype(BF16) for _, slot in lines]


def expert_onehots(lines, experts):
    tok = lines[0][0].shape[1]
    diagonal = iota((tok, tok), 0) == iota((tok, tok), 1)
    found = []
    for expert, _ in lines:
        column = jnp.sum(jnp.where(diagonal, expert, 0.0), axis=1, keepdims=True)
        found.append(iota((tok, experts), 1) == column.astype(jnp.int32))
    return found


def attend_body(head_width, off_ref, qkv_ref, out_ref):
    frames = qkv_ref.shape[0]
    q, k, v = [rows_of(qkv_ref[:, 8 * s : 8 * s + 8, :]).astype(BF16) for s in range(3)]
    rows = frames * 8
    off = off_ref[0]
    same = (
        lax.broadcasted_iota(jnp.int32, (rows, rows), 0) & 7
    ) == (lax.broadcasted_iota(jnp.int32, (rows, rows), 1) & 7)
    lane = lax.broadcasted_iota(jnp.int32, (rows, 256), 1)
    tiles = [jnp.zeros((rows, 128), F32) for _ in range(WIDE // 128)]
    for h in range(H // 2):
        w = h // 2
        first = off + head_width * h - 128 * w
        inside = (lane >= first) & (lane < first + head_width)
        cols = slice(128 * w, 128 * w + 256)
        mine = jnp.where(inside, q[:, cols].astype(F32), 0.0).astype(BF16)
        scores = lax.dot_general(
            mine, k[:, cols], (((1,), (1,)), ((), ())), preferred_element_type=F32
        ) * head_width ** (-0.5)
        scores = jnp.where(same, scores, -1e30)
        peak = jnp.max(scores, axis=1, keepdims=True)
        weights = jnp.exp(scores - peak)
        probs = (weights / jnp.sum(weights, axis=1, keepdims=True)).astype(BF16)
        got = jnp.dot(probs, v[:, cols], preferred_element_type=F32)
        for t in range(2):
            part = slice(128 * t, 128 * t + 128)
            tiles[w + t] = jnp.where(inside[:, part], got[:, part], tiles[w + t])
    for t, tile in enumerate(tiles):
        out_ref[:, :, 128 * t : 128 * t + 128] = blocks_of(tile)


def inv_rms_of(hidden_float):
    return lax.rsqrt(jnp.mean(hidden_float * hidden_float, axis=-1, keepdims=True) + 1e-06)


def project_body(
    att_ref, residual_ref, w_out_ref, gain_ref, w_router_ref, routes_ref, cot_ref,
    hidden_ref, combine_ref, out_ref,
):
    low, high = rows_of(att_ref[:, 0]), rows_of(att_ref[:, 1])
    shared = WIDE - STEP
    attended = jnp.concatenate(
        [low[:, :STEP], low[:, STEP:] + high[:, :shared], high[:, shared:]], axis=1
    ).astype(BF16)
    stream = residual_ref[...].astype(F32) + jnp.dot(
        attended, w_out_ref[...], preferred_element_type=F32
    )
    hidden = stream.astype(BF16)
    hidden_ref[...] = hidden
    hidden_float = hidden.astype(F32)
    normed = (hidden_float * inv_rms_of(hidden_float) * gain_ref[...]).astype(BF16)
    chips, _, planes, cap, width = out_ref.shape
    experts = chips * planes
    lines = slot_lines(routes_ref, experts, cap)
    picks = slot_onehots(lines, experts * cap)
    picks = picks[0] + picks[1]
    step = 4
    for core, rows in enumerate((normed, cot_ref[...])):
        for at in range(0, chips, step):
            some = picks[at * planes * cap : (at + step) * planes * cap]
            blocks = blocks_of(jnp.dot(some, rows, preferred_element_type=F32))
            out_ref[at : at + step, core] = blocks.reshape(step, planes, cap, width)
    logits = jnp.dot(normed, w_router_ref[...], preferred_element_type=F32)
    for j, onehot in enumerate(expert_onehots(lines, experts)):
        chosen = jnp.sum(jnp.where(onehot, logits, 0.0), axis=1, keepdims=True)
        combine_ref[:, j : j + 1] = jax.nn.sigmoid(chosen)


def expert_body(
    state_ref, here_ref, there_ref, column_ref,
    home_gate_ref, home_up_ref, home_down_ref, new_gate_ref, new_up_ref, new_down_ref,
    keep_ref, send_ref, scaled_ref, units_ref, d_gate_ref, d_up_ref,
    gate_ref, up_ref, down_ref, sems,
):
    turned = (((1,), (1,)), ((), ()))
    first, moved = state_ref[0] == 0, state_ref[1] == 1
    opening = pl.program_id(0) == 0
    targets = (gate_ref, up_ref, down_ref)

    def fetch(sources):
        for n, (source, target) in enumerate(zip(sources, targets)):
            pltpu.make_async_copy(source, target, sems.at[n]).start()

    @pl.when(opening & moved)
    def _():
        fetch((new_gate_ref, new_up_ref, new_down_ref))

    @pl.when(opening & jnp.logical_not(moved))
    def _():
        fetch((home_gate_ref, home_up_ref, home_down_ref))

    def arrived(n):
        @pl.when(opening)
        def _():
            pltpu.make_async_copy(home_gate_ref if n < 2 else home_down_ref, targets[n],
                                  sems.at[n]).wait()

    def work(rows_ref, cot_ref, out_ref, in_ref):
        x = rows_ref[...]
        arrived(0)
        pre_gate = jnp.dot(x, gate_ref[0], preferred_element_type=F32)
        arrived(1)
        pre_up = jnp.dot(x, up_ref[0], preferred_element_type=F32)
        gate_sig = jax.nn.sigmoid(pre_gate)
        gate_act = pre_gate * gate_sig
        units = (gate_act * pre_up).astype(BF16)
        units_ref[...] = units
        arrived(2)
        out_ref[...] = jnp.dot(units, down_ref[0], preferred_element_type=F32).astype(BF16)
        chosen = jnp.sum(x.astype(F32) * column_ref[...], axis=1, keepdims=True)
        scaled = (jax.nn.sigmoid(chosen) * cot_ref[...].astype(F32)).astype(BF16)
        scaled_ref[...] = scaled
        d_units = lax.dot_general(scaled, down_ref[0], turned, preferred_element_type=F32)
        slope = pre_up * (gate_sig + gate_act * (1.0 - gate_sig))
        d_pre_gate = (d_units * slope).astype(BF16)
        d_pre_up = (d_units * gate_act).astype(BF16)
        d_gate_ref[...] = d_pre_gate
        d_up_ref[...] = d_pre_up
        in_ref[...] = (
            lax.dot_general(d_pre_gate, gate_ref[0], turned, preferred_element_type=F32)
            + lax.dot_general(d_pre_up, up_ref[0], turned, preferred_element_type=F32)
        ).astype(BF16)

    @pl.when(first)
    def _():
        work(here_ref, there_ref, keep_ref, send_ref)

    @pl.when(jnp.logical_not(first))
    def _():
        work(there_ref, here_ref, send_ref, keep_ref)


def down_body(units_ref, scaled_ref, out_ref):
    out_ref[0] = lax.dot_general(
        units_ref[...], scaled_ref[...], (((0,), (0,)), ((), ())), preferred_element_type=F32
    ).astype(BF16)


def gates_body(state_ref, here_ref, there_ref, left_ref, right_ref, gate_ref, up_ref):
    def work(x_ref):
        for ref, out_ref in ((left_ref, gate_ref), (right_ref, up_ref)):
            out_ref[0] = lax.dot_general(
                x_ref[...], ref[...], (((0,), (0,)), ((), ())), preferred_element_type=F32
            ).astype(BF16)

    for core, x_ref in enumerate((here_ref, there_ref)):
        pl.when(state_ref[0] == core)(functools.partial(work, x_ref))


def widen_body(state_ref, home_ref, new_ref, out_ref):
    out_ref[...] = jnp.where(state_ref[1] == 1, new_ref[...], home_ref[...]).astype(F32)


def spread(onehot, rows):
    return lax.dot_general(onehot, rows, (((0,), (0,)), ((), ())), preferred_element_type=F32)


def finish_body(
    back_ref, routes_ref, combine_ref, cot_ref, hidden_ref, gain_ref, w_router_ref,
    block_ref, d_hidden_ref, got_ref,
):
    chips, _, planes, cap, width = back_ref.shape
    experts = chips * planes
    tok = hidden_ref.shape[0]
    lines = slot_lines(routes_ref, experts, cap)
    picks = slot_onehots(lines, experts * cap)
    either = picks[0] + picks[1]
    combines = [combine_ref[:, j : j + 1] for j in range(2)]
    d_combines = [jnp.zeros((tok, 1), F32) for _ in range(2)]
    for at in range(0, width, 384):
        cols = slice(at, at + 384)
        outs, ins = [
            rows_of(back_ref[:, core, :, :, cols].reshape(experts, cap, 384)).astype(BF16)
            for core in range(2)
        ]
        got_ref[:, cols] = spread(either, ins)
        cotangent = cot_ref[:, cols].astype(F32)
        block = hidden_ref[:, cols].astype(F32)
        for j in range(2):
            expert_out = spread(picks[j], outs)
            block = block + combines[j] * expert_out
            d_combines[j] = d_combines[j] + jnp.sum(
                cotangent * expert_out, axis=1, keepdims=True
            )
        block_ref[:, cols] = block.astype(BF16)
    rows = jnp.zeros((tok, experts), F32)
    for j, onehot in enumerate(expert_onehots(lines, experts)):
        d_logit = d_combines[j] * combines[j] * (1.0 - combines[j])
        rows = rows + jnp.where(onehot, d_logit, 0.0)
    d_normed = got_ref[...] + lax.dot_general(
        rows,
        w_router_ref[...].astype(F32),
        (((1,), (1,)), ((), ())),
        precision=lax.Precision.HIGHEST,
        preferred_element_type=F32,
    )
    hidden_float = hidden_ref[...].astype(F32)
    inv_rms = inv_rms_of(hidden_float)
    gained = d_normed * gain_ref[...]
    d_norm_in = inv_rms * gained - hidden_float * inv_rms**3 * jnp.mean(
        gained * hidden_float, axis=-1, keepdims=True
    )
    d_hidden_ref[...] = (cot_ref[...].astype(F32) + d_norm_in).astype(BF16)


def relay(parcel, axes):
    return lax.all_to_all(parcel, axes, split_axis=0, concat_axis=0, tiled=True)


def on_device(
    residual, queries, keys_in, values, w_out, norm_gain, w_router, routes, w_gate, w_up, w_down,
    d_out,
):
    everyone = ("frames", "expert")
    frames = lax.axis_size("frames")
    planes = lax.axis_size("expert")
    devices = frames * planes
    chips = frames // 2
    width = residual.shape[2]
    tok = residual.shape[0] * residual.shape[1]
    experts = w_router.shape[1]
    cap = 4 * tok // experts
    slots = experts * cap
    hidden_units = w_gate.shape[2]
    smem = pl.BlockSpec(memory_space=pltpu.SMEM)
    fixed = lambda *dims: pl.BlockSpec(dims, lambda i: (0,) * len(dims))
    whole = lambda a: fixed(*a.shape)
    flat = lambda a: a.reshape(tok, width)
    eights = lambda a: a.reshape(tok // 8, 8, width)
    cot = flat(d_out)
    pairs = jnp.swapaxes(routes.reshape(tok, 2), 0, 1)
    gain = norm_gain.reshape(1, width)
    me, plane = lax.axis_index("frames"), lax.axis_index("expert")
    core = me % 2
    offset = (core * (width // 2 - STEP)).reshape(1)
    mine = 4 * (me // 2) + 2 * (plane % 2) + plane // 2
    column = lax.dynamic_slice(w_router, (0, mine), (width, 1)).astype(F32).reshape(1, width)
    swaps = [
        (f * planes + z, (f ^ 1) * planes + (z ^ 1))
        for f in range(frames)
        for z in range(planes)
        if (f + z) % 2
    ]
    state = jnp.stack([core, (me + plane) % 2]).astype(jnp.int32)
    swap = lambda a: lax.ppermute(a, everyone, swaps)
    beside = lambda a: lax.ppermute(a, "frames", [(i, i ^ 1) for i in range(frames)])

    moved_w = [swap(w) for w in (w_gate, w_up, w_down)]
    part = tok // 32
    packed = call(
        pack_body,
        shape((chips, 2, 24, WIDE), BF16),
        (0, 2 * frames * 24 * WIDE * 2),
        limit=ROOMY,
        grid=(4,),
        in_specs=[pl.BlockSpec((part, 8, width), lambda i: (i, 0, 0))] * 3,
        out_specs=pl.BlockSpec((part, 2, 24, WIDE), lambda i: (i, 0, 0, 0)),
    )(eights(queries), eights(keys_in), eights(values))
    qkv = relay(packed.reshape(frames, 24, WIDE), "frames")
    attended = call(
        lambda *refs: attend_body(width // H, *refs),
        shape((frames, 8, WIDE), BF16),
        (1 << 29, 4 * frames * 8 * WIDE * 2),
        grid=(1,),
        in_specs=[smem, fixed(frames, 24, WIDE)],
        out_specs=fixed(frames, 8, WIDE),
    )(offset, qkv)
    attended = relay(attended, "frames").reshape(chips, 2, 8, WIDE)
    hidden, combine, outbound = call(
        project_body,
        (shape((tok, width), BF16), shape((tok, 2), F32),
         shape((chips, 2, planes, cap, width), BF16)),
        (2 * tok * width * (width + 2 * slots), (width + 3 * slots) * width * 2),
        grid=(1,),
        in_specs=[whole(attended), whole(cot), whole(w_out), whole(gain), whole(w_router),
                  whole(pairs), whole(cot)],
        out_specs=(whole(cot), fixed(tok, 2), fixed(chips, 2, planes, cap, width)),
    )(attended, flat(residual), w_out, gain, w_router, pairs, cot)
    outbound, *moved_w = lax.optimization_barrier((outbound, *moved_w))
    here = relay(outbound.reshape(devices, cap, width), everyone)
    there = beside(here)

    total = devices * cap
    block = 512
    by_rows = lambda w: pl.BlockSpec((block, w), lambda i: (i, 0))
    rows = lambda a: a.reshape(total, width)
    product = 2 * total * width * hidden_units
    wide = shape((total, width), BF16)
    inner = shape((total, hidden_units), BF16)
    hbm = pl.BlockSpec(memory_space=pltpu.HBM)
    keep, send, scaled, units, d_pre_gate, d_pre_up = call(
        expert_body,
        (wide, wide, wide, inner, inner, inner),
        (6 * product, 10 * total * width * 2),
        limit=ROOMY,
        grid=(total // block,),
        in_specs=[smem, by_rows(width), by_rows(width), whole(column)] + [hbm] * 6,
        out_specs=[by_rows(width)] * 3 + [by_rows(hidden_units)] * 3,
        scratch_shapes=[
            pltpu.VMEM(w_gate.shape, BF16),
            pltpu.VMEM(w_up.shape, BF16),
            pltpu.VMEM(w_down.shape, BF16),
            pltpu.SemaphoreType.DMA((3,)),
        ],
    )(state, rows(here), rows(there), column, w_gate, w_up, w_down, *moved_w)
    got = beside(send)
    third = width // 3
    half = hidden_units // 2

    def down_rows(n):
        return call(
            down_body,
            shape((1, half, width), BF16),
            (product // 2, 2 * total * width * 2),
            limit=ROOMY,
            grid=(1,),
            in_specs=[pl.BlockSpec((total, half), lambda i: (0, n)), whole(scaled)],
            out_specs=fixed(1, half, width),
        )(units, scaled)

    upper = down_rows(0)
    new_upper = swap(upper)
    lower = down_rows(1)
    got, lower = lax.optimization_barrier((got, lower))
    returned = (keep.astype(F32) + got.astype(F32)).astype(BF16)
    returned, new_upper = lax.optimization_barrier((returned, new_upper))
    back = relay(returned.reshape(devices, cap, width), everyone)
    back = back.reshape(chips, 2, planes, cap, width)

    def chosen(core_index):
        return lambda i, state: (0, jnp.where(state[0] == core_index, i, 0))

    still = lambda i, state: (0, 0)
    d_gate, d_up = pl.pallas_call(
        gates_body,
        out_shape=(shape(w_gate.shape, BF16), shape(w_up.shape, BF16)),
        grid_spec=pltpu.PrefetchScalarGridSpec(
            num_scalar_prefetch=1,
            grid=(3,),
            in_specs=[
                pl.BlockSpec((total, third), chosen(0)),
                pl.BlockSpec((total, third), chosen(1)),
                pl.BlockSpec((total, hidden_units), still),
                pl.BlockSpec((total, hidden_units), still),
            ],
            out_specs=[pl.BlockSpec((1, third, hidden_units), lambda i, state: (0, i, 0))] * 2,
        ),
        compiler_params=pltpu.CompilerParams(vmem_limit_bytes=ROOMY),
        cost_estimate=pl.CostEstimate(
            flops=2 * product, bytes_accessed=4 * total * width * 2, transcendentals=0
        ),
    )(state, rows(here), rows(there), d_pre_gate, d_pre_up)

    def widen(home, new):
        _, height, across = home.shape
        part = height // 4
        pick = lambda n: lambda i, state: (0, jnp.where(state[1] == n, i, 0), 0)
        return pl.pallas_call(
            widen_body,
            out_shape=shape(home.shape, F32),
            grid_spec=pltpu.PrefetchScalarGridSpec(
                num_scalar_prefetch=1,
                grid=(4,),
                in_specs=[pl.BlockSpec((1, part, across), pick(n)) for n in range(2)],
                out_specs=pl.BlockSpec((1, part, across), lambda i, state: (0, i, 0)),
            ),
            compiler_params=pltpu.CompilerParams(vmem_limit_bytes=SNUG),
            cost_estimate=pl.CostEstimate(
                flops=height * across, bytes_accessed=6 * height * across, transcendentals=0
            ),
        )(state, home, new)

    new_lower = swap(lower)
    new_gate = swap(d_gate)
    d_up, new_lower = lax.optimization_barrier((d_up, new_lower))
    new_up = swap(d_up)
    block_out, d_hidden = call(
        finish_body,
        (shape((tok, width), BF16), shape((tok, width), BF16)),
        (6 * tok * width * slots, 4 * slots * width * 2),
        limit=ROOMY,
        grid=(1,),
        in_specs=[whole(back), whole(pairs), whole(combine), whole(cot), whole(hidden),
                  whole(gain), whole(w_router)],
        out_specs=(whole(cot), whole(cot)),
        scratch_shapes=[pltpu.VMEM((tok, width), F32)],
    )(back, pairs, combine, cot, hidden, gain, w_router)
    new_up, d_hidden = lax.optimization_barrier((new_up, d_hidden))
    upper, lower, d_gate, d_up = [
        widen(*pair)
        for pair in (
            (upper, new_upper), (lower, new_lower), (d_gate, new_gate), (d_up, new_up)
        )
    ]
    d_down = jnp.concatenate([upper, lower], axis=1)
    return (
        block_out.reshape(residual.shape),
        d_hidden.reshape(residual.shape),
        d_gate,
        d_up,
        d_down,
    )


def solution(mesh):
    tokens = P("frames", "expert", None)
    weights = P(("frames", "expert"), None, None)
    return jax.shard_map(
        on_device,
        mesh=mesh,
        in_specs=(tokens,) * 4
        + (P(), P(), P(), P("expert", "frames", None, None))
        + (weights,) * 3
        + (tokens,),
        out_specs=(tokens, tokens, weights, weights, weights),
        check_vma=False,
    )
```

```python
import functools

import jax
import jax.numpy as jnp
from jax import lax
from jax.experimental import pallas as pl
from jax.experimental.pallas import tpu as pltpu
from jax.sharding import PartitionSpec as P

H = 16
F32 = jnp.float32
BF16 = jnp.bfloat16
WIDE = 640
STEP = 512
ROOMY = 60 * 1024 * 1024
SNUG = 32 * 1024 * 1024


def call(body, outs, cost, limit=SNUG, **extra):
    flops, moved = cost
    return pl.pallas_call(
        body,
        out_shape=outs,
        compiler_params=pltpu.CompilerParams(vmem_limit_bytes=limit),
        cost_estimate=pl.CostEstimate(flops=flops, bytes_accessed=moved, transcendentals=0),
        **extra,
    )


def shape(dims, dtype):
    return jax.ShapeDtypeStruct(dims, dtype)


def rows_of(blocks):
    n, eight, width = blocks.shape
    return blocks.astype(F32).reshape(n * eight, width)


def blocks_of(rows):
    total, width = rows.shape
    return rows.reshape(total // 8, 8, width).astype(BF16)


def pack_body(q_ref, k_ref, v_ref, out_ref):
    for s, ref in enumerate((q_ref, k_ref, v_ref)):
        for i in range(ref.shape[0]):
            for half in range(2):
                out_ref[i, half, 8 * s : 8 * s + 8, :] = ref[
                    i, :, STEP * half : STEP * half + WIDE
                ]


def iota(dims, axis):
    return lax.broadcasted_iota(jnp.int32, dims, axis)


def slot_lines(routes_ref, experts, cap):
    tok = routes_ref.shape[1]
    lines = [routes_ref[j : j + 1, :] for j in range(2)]
    onehots = [iota((experts, tok), 0) == line for line in lines]
    named = jnp.where(onehots[0] | onehots[1], 1.0, 0.0).astype(BF16)
    later = jnp.where(iota((tok, tok), 0) < iota((tok, tok), 1), 1.0, 0.0).astype(BF16)
    before = jnp.dot(named, later, preferred_element_type=F32)
    found = []
    for line, onehot in zip(lines, onehots):
        rank = jnp.sum(jnp.where(onehot, before, 0.0), axis=0, keepdims=True)
        place = (line & -4) | ((line & 1) << 1) | ((line >> 1) & 1)
        found.append((line.astype(F32), place.astype(F32) * cap + rank))
    return found


def slot_onehots(lines, slots):
    where = iota((slots, lines[0][1].shape[1]), 0).astype(F32)
    return [jnp.where(where == slot, 1.0, 0.0).astype(BF16) for _, slot in lines]


def expert_onehots(lines, experts):
    tok = lines[0][0].shape[1]
    diagonal = iota((tok, tok), 0) == iota((tok, tok), 1)
    found = []
    for expert, _ in lines:
        column = jnp.sum(jnp.where(diagonal, expert, 0.0), axis=1, keepdims=True)
        found.append(iota((tok, experts), 1) == column.astype(jnp.int32))
    return found


def attend_body(head_width, off_ref, qkv_ref, out_ref):
    frames = qkv_ref.shape[0]
    q, k, v = [rows_of(qkv_ref[:, 8 * s : 8 * s + 8, :]).astype(BF16) for s in range(3)]
    rows = frames * 8
    off = off_ref[0]
    same = (
        lax.broadcasted_iota(jnp.int32, (rows, rows), 0) & 7
    ) == (lax.broadcasted_iota(jnp.int32, (rows, rows), 1) & 7)
    lane = lax.broadcasted_iota(jnp.int32, (rows, 256), 1)
    tiles = [jnp.zeros((rows, 128), F32) for _ in range(WIDE // 128)]
    for h in range(H // 2):
        w = h // 2
        first = off + head_width * h - 128 * w
        inside = (lane >= first) & (lane < first + head_width)
        cols = slice(128 * w, 128 * w + 256)
        mine = jnp.where(inside, q[:, cols].astype(F32), 0.0).astype(BF16)
        scores = lax.dot_general(
            mine, k[:, cols], (((1,), (1,)), ((), ())), preferred_element_type=F32
        ) * head_width ** (-0.5)
        scores = jnp.where(same, scores, -1e30)
        peak = jnp.max(scores, axis=1, keepdims=True)
        weights = jnp.exp(scores - peak)
        probs = (weights / jnp.sum(weights, axis=1, keepdims=True)).astype(BF16)
        got = jnp.dot(probs, v[:, cols], preferred_element_type=F32)
        for t in range(2):
            part = slice(128 * t, 128 * t + 128)
            tiles[w + t] = jnp.where(inside[:, part], got[:, part], tiles[w + t])
    for t, tile in enumerate(tiles):
        out_ref[:, :, 128 * t : 128 * t + 128] = blocks_of(tile)


def inv_rms_of(hidden_float):
    return lax.rsqrt(jnp.mean(hidden_float * hidden_float, axis=-1, keepdims=True) + 1e-06)


def project_body(
    att_ref, residual_ref, w_out_ref, gain_ref, w_router_ref, routes_ref, cot_ref,
    hidden_ref, combine_ref, out_ref,
):
    low, high = rows_of(att_ref[:, 0]), rows_of(att_ref[:, 1])
    shared = WIDE - STEP
    attended = jnp.concatenate(
        [low[:, :STEP], low[:, STEP:] + high[:, :shared], high[:, shared:]], axis=1
    ).astype(BF16)
    stream = residual_ref[...].astype(F32) + jnp.dot(
        attended, w_out_ref[...], preferred_element_type=F32
    )
    hidden = stream.astype(BF16)
    hidden_ref[...] = hidden
    hidden_float = hidden.astype(F32)
    normed = (hidden_float * inv_rms_of(hidden_float) * gain_ref[...]).astype(BF16)
    chips, _, planes, cap, width = out_ref.shape
    experts = chips * planes
    lines = slot_lines(routes_ref, experts, cap)
    picks = slot_onehots(lines, experts * cap)
    picks = picks[0] + picks[1]
    step = 4
    for core, rows in enumerate((normed, cot_ref[...])):
        for at in range(0, chips, step):
            some = picks[at * planes * cap : (at + step) * planes * cap]
            blocks = blocks_of(jnp.dot(some, rows, preferred_element_type=F32))
            out_ref[at : at + step, core] = blocks.reshape(step, planes, cap, width)
    logits = jnp.dot(normed, w_router_ref[...], preferred_element_type=F32)
    for j, onehot in enumerate(expert_onehots(lines, experts)):
        chosen = jnp.sum(jnp.where(onehot, logits, 0.0), axis=1, keepdims=True)
        combine_ref[:, j : j + 1] = jax.nn.sigmoid(chosen)


def expert_body(
    state_ref, here_ref, there_ref, column_ref,
    home_gate_ref, home_up_ref, home_down_ref, new_gate_ref, new_up_ref, new_down_ref,
    keep_ref, send_ref, scaled_ref, units_ref, d_gate_ref, d_up_ref,
    gate_ref, up_ref, down_ref, sems,
):
    turned = (((1,), (1,)), ((), ()))
    first, moved = state_ref[0] == 0, state_ref[1] == 1
    opening = pl.program_id(0) == 0
    targets = (gate_ref, up_ref, down_ref)

    def fetch(sources):
        for n, (source, target) in enumerate(zip(sources, targets)):
            pltpu.make_async_copy(source, target, sems.at[n]).start()

    @pl.when(opening & moved)
    def _():
        fetch((new_gate_ref, new_up_ref, new_down_ref))

    @pl.when(opening & jnp.logical_not(moved))
    def _():
        fetch((home_gate_ref, home_up_ref, home_down_ref))

    def arrived(n):
        @pl.when(opening)
        def _():
            pltpu.make_async_copy(home_gate_ref if n < 2 else home_down_ref, targets[n],
                                  sems.at[n]).wait()

    def work(rows_ref, cot_ref, out_ref, in_ref):
        x = rows_ref[...]
        arrived(0)
        pre_gate = jnp.dot(x, gate_ref[0], preferred_element_type=F32)
        arrived(1)
        pre_up = jnp.dot(x, up_ref[0], preferred_element_type=F32)
        gate_sig = jax.nn.sigmoid(pre_gate)
        gate_act = pre_gate * gate_sig
        units = (gate_act * pre_up).astype(BF16)
        units_ref[...] = units
        arrived(2)
        out_ref[...] = jnp.dot(units, down_ref[0], preferred_element_type=F32).astype(BF16)
        chosen = jnp.sum(x.astype(F32) * column_ref[...], axis=1, keepdims=True)
        scaled = (jax.nn.sigmoid(chosen) * cot_ref[...].astype(F32)).astype(BF16)
        scaled_ref[...] = scaled
        d_units = lax.dot_general(scaled, down_ref[0], turned, preferred_element_type=F32)
        slope = pre_up * (gate_sig + gate_act * (1.0 - gate_sig))
        d_pre_gate = (d_units * slope).astype(BF16)
        d_pre_up = (d_units * gate_act).astype(BF16)
        d_gate_ref[...] = d_pre_gate
        d_up_ref[...] = d_pre_up
        in_ref[...] = (
            lax.dot_general(d_pre_gate, gate_ref[0], turned, preferred_element_type=F32)
            + lax.dot_general(d_pre_up, up_ref[0], turned, preferred_element_type=F32)
        ).astype(BF16)

    @pl.when(first)
    def _():
        work(here_ref, there_ref, keep_ref, send_ref)

    @pl.when(jnp.logical_not(first))
    def _():
        work(there_ref, here_ref, send_ref, keep_ref)


def down_body(units_ref, scaled_ref, out_ref):
    out_ref[0] = lax.dot_general(
        units_ref[...], scaled_ref[...], (((0,), (0,)), ((), ())), preferred_element_type=F32
    ).astype(BF16)


def gates_body(state_ref, here_ref, there_ref, left_ref, right_ref, gate_ref, up_ref):
    def work(x_ref):
        for ref, out_ref in ((left_ref, gate_ref), (right_ref, up_ref)):
            out_ref[0] = lax.dot_general(
                x_ref[...], ref[...], (((0,), (0,)), ((), ())), preferred_element_type=F32
            ).astype(BF16)

    for core, x_ref in enumerate((here_ref, there_ref)):
        pl.when(state_ref[0] == core)(functools.partial(work, x_ref))


def widen_body(state_ref, home_ref, new_ref, out_ref):
    out_ref[...] = jnp.where(state_ref[1] == 1, new_ref[...], home_ref[...]).astype(F32)


def spread(onehot, rows):
    return lax.dot_general(onehot, rows, (((0,), (0,)), ((), ())), preferred_element_type=F32)


def finish_body(
    back_ref, routes_ref, combine_ref, cot_ref, hidden_ref, gain_ref, w_router_ref,
    block_ref, d_hidden_ref, got_ref,
):
    chips, _, planes, cap, width = back_ref.shape
    experts = chips * planes
    tok = hidden_ref.shape[0]
    lines = slot_lines(routes_ref, experts, cap)
    picks = slot_onehots(lines, experts * cap)
    either = picks[0] + picks[1]
    combines = [combine_ref[:, j : j + 1] for j in range(2)]
    d_combines = [jnp.zeros((tok, 1), F32) for _ in range(2)]
    for at in range(0, width, 384):
        cols = slice(at, at + 384)
        outs, ins = [
            rows_of(back_ref[:, core, :, :, cols].reshape(experts, cap, 384)).astype(BF16)
            for core in range(2)
        ]
        got_ref[:, cols] = spread(either, ins)
        cotangent = cot_ref[:, cols].astype(F32)
        block = hidden_ref[:, cols].astype(F32)
        for j in range(2):
            expert_out = spread(picks[j], outs)
            block = block + combines[j] * expert_out
            d_combines[j] = d_combines[j] + jnp.sum(
                cotangent * expert_out, axis=1, keepdims=True
            )
        block_ref[:, cols] = block.astype(BF16)
    rows = jnp.zeros((tok, experts), F32)
    for j, onehot in enumerate(expert_onehots(lines, experts)):
        d_logit = d_combines[j] * combines[j] * (1.0 - combines[j])
        rows = rows + jnp.where(onehot, d_logit, 0.0)
    d_normed = got_ref[...] + lax.dot_general(
        rows,
        w_router_ref[...].astype(F32),
        (((1,), (1,)), ((), ())),
        precision=lax.Precision.HIGHEST,
        preferred_element_type=F32,
    )
    hidden_float = hidden_ref[...].astype(F32)
    inv_rms = inv_rms_of(hidden_float)
    gained = d_normed * gain_ref[...]
    d_norm_in = inv_rms * gained - hidden_float * inv_rms**3 * jnp.mean(
        gained * hidden_float, axis=-1, keepdims=True
    )
    d_hidden_ref[...] = (cot_ref[...].astype(F32) + d_norm_in).astype(BF16)


def relay(parcel, axes):
    return lax.all_to_all(parcel, axes, split_axis=0, concat_axis=0, tiled=True)


def on_device(
    residual, queries, keys_in, values, w_out, norm_gain, w_router, routes, w_gate, w_up, w_down,
    d_out,
):
    everyone = ("frames", "expert")
    frames = lax.axis_size("frames")
    planes = lax.axis_size("expert")
    devices = frames * planes
    chips = frames // 2
    width = residual.shape[2]
    tok = residual.shape[0] * residual.shape[1]
    experts = w_router.shape[1]
    cap = 4 * tok // experts
    slots = experts * cap
    hidden_units = w_gate.shape[2]
    smem = pl.BlockSpec(memory_space=pltpu.SMEM)
    fixed = lambda *dims: pl.BlockSpec(dims, lambda i: (0,) * len(dims))
    whole = lambda a: fixed(*a.shape)
    flat = lambda a: a.reshape(tok, width)
    eights = lambda a: a.reshape(tok // 8, 8, width)
    cot = flat(d_out)
    pairs = jnp.swapaxes(routes.reshape(tok, 2), 0, 1)
    gain = norm_gain.reshape(1, width)
    me, plane = lax.axis_index("frames"), lax.axis_index("expert")
    core = me % 2
    offset = (core * (width // 2 - STEP)).reshape(1)
    mine = 4 * (me // 2) + 2 * (plane % 2) + plane // 2
    column = lax.dynamic_slice(w_router, (0, mine), (width, 1)).astype(F32).reshape(1, width)
    swaps = [
        (f * planes + z, (f ^ 1) * planes + (z ^ 1))
        for f in range(frames)
        for z in range(planes)
        if (f + z) % 2
    ]
    state = jnp.stack([core, (me + plane) % 2]).astype(jnp.int32)
    swap = lambda a: lax.ppermute(a, everyone, swaps)
    beside = lambda a: lax.ppermute(a, "frames", [(i, i ^ 1) for i in range(frames)])

    moved_w = [swap(w) for w in (w_gate, w_up, w_down)]
    part = tok // 32
    packed = call(
        pack_body,
        shape((chips, 2, 24, WIDE), BF16),
        (0, 2 * frames * 24 * WIDE * 2),
        limit=ROOMY,
        grid=(4,),
        in_specs=[pl.BlockSpec((part, 8, width), lambda i: (i, 0, 0))] * 3,
        out_specs=pl.BlockSpec((part, 2, 24, WIDE), lambda i: (i, 0, 0, 0)),
    )(eights(queries), eights(keys_in), eights(values))
    qkv = relay(packed.reshape(frames, 24, WIDE), "frames")
    attended = call(
        lambda *refs: attend_body(width // H, *refs),
        shape((frames, 8, WIDE), BF16),
        (1 << 29, 4 * frames * 8 * WIDE * 2),
        grid=(1,),
        in_specs=[smem, fixed(frames, 24, WIDE)],
        out_specs=fixed(frames, 8, WIDE),
    )(offset, qkv)
    attended = relay(attended, "frames").reshape(chips, 2, 8, WIDE)
    hidden, combine, outbound = call(
        project_body,
        (shape((tok, width), BF16), shape((tok, 2), F32),
         shape((chips, 2, planes, cap, width), BF16)),
        (2 * tok * width * (width + 2 * slots), (width + 3 * slots) * width * 2),
        grid=(1,),
        in_specs=[whole(attended), whole(cot), whole(w_out), whole(gain), whole(w_router),
                  whole(pairs), whole(cot)],
        out_specs=(whole(cot), fixed(tok, 2), fixed(chips, 2, planes, cap, width)),
    )(attended, flat(residual), w_out, gain, w_router, pairs, cot)
    outbound, *moved_w = lax.optimization_barrier((outbound, *moved_w))
    here = relay(outbound.reshape(devices, cap, width), everyone)
    there = beside(here)

    total = devices * cap
    block = 512
    by_rows = lambda w: pl.BlockSpec((block, w), lambda i: (i, 0))
    rows = lambda a: a.reshape(total, width)
    product = 2 * total * width * hidden_units
    wide = shape((total, width), BF16)
    inner = shape((total, hidden_units), BF16)
    hbm = pl.BlockSpec(memory_space=pltpu.HBM)
    keep, send, scaled, units, d_pre_gate, d_pre_up = call(
        expert_body,
        (wide, wide, wide, inner, inner, inner),
        (6 * product, 10 * total * width * 2),
        limit=ROOMY,
        grid=(total // block,),
        in_specs=[smem, by_rows(width), by_rows(width), whole(column)] + [hbm] * 6,
        out_specs=[by_rows(width)] * 3 + [by_rows(hidden_units)] * 3,
        scratch_shapes=[
            pltpu.VMEM(w_gate.shape, BF16),
            pltpu.VMEM(w_up.shape, BF16),
            pltpu.VMEM(w_down.shape, BF16),
            pltpu.SemaphoreType.DMA((3,)),
        ],
    )(state, rows(here), rows(there), column, w_gate, w_up, w_down, *moved_w)
    got = beside(send)
    third = width // 3
    half = hidden_units // 2

    def down_rows(n):
        return call(
            down_body,
            shape((1, half, width), BF16),
            (product // 2, 2 * total * width * 2),
            limit=ROOMY,
            grid=(1,),
            in_specs=[pl.BlockSpec((total, half), lambda i: (0, n)), whole(scaled)],
            out_specs=fixed(1, half, width),
        )(units, scaled)

    upper = down_rows(0)
    new_upper = swap(upper)
    lower = down_rows(1)
    got, lower = lax.optimization_barrier((got, lower))
    returned = (keep.astype(F32) + got.astype(F32)).astype(BF16)
    returned, new_upper = lax.optimization_barrier((returned, new_upper))
    back = relay(returned.reshape(devices, cap, width), everyone)
    back = back.reshape(chips, 2, planes, cap, width)

    def chosen(core_index):
        return lambda i, state: (0, jnp.where(state[0] == core_index, i, 0))

    still = lambda i, state: (0, 0)
    d_gate, d_up = pl.pallas_call(
        gates_body,
        out_shape=(shape(w_gate.shape, BF16), shape(w_up.shape, BF16)),
        grid_spec=pltpu.PrefetchScalarGridSpec(
            num_scalar_prefetch=1,
            grid=(3,),
            in_specs=[
                pl.BlockSpec((total, third), chosen(0)),
                pl.BlockSpec((total, third), chosen(1)),
                pl.BlockSpec((total, hidden_units), still),
                pl.BlockSpec((total, hidden_units), still),
            ],
            out_specs=[pl.BlockSpec((1, third, hidden_units), lambda i, state: (0, i, 0))] * 2,
        ),
        compiler_params=pltpu.CompilerParams(vmem_limit_bytes=ROOMY),
        cost_estimate=pl.CostEstimate(
            flops=2 * product, bytes_accessed=4 * total * width * 2, transcendentals=0
        ),
    )(state, rows(here), rows(there), d_pre_gate, d_pre_up)

    def widen(home, new):
        _, height, across = home.shape
        part = height // 8
        pick = lambda n: lambda i, state: (0, jnp.where(state[1] == n, i, 0), 0)
        return pl.pallas_call(
            widen_body,
            out_shape=shape(home.shape, F32),
            grid_spec=pltpu.PrefetchScalarGridSpec(
                num_scalar_prefetch=1,
                grid=(8,),
                in_specs=[pl.BlockSpec((1, part, across), pick(n)) for n in range(2)],
                out_specs=pl.BlockSpec((1, part, across), lambda i, state: (0, i, 0)),
            ),
            compiler_params=pltpu.CompilerParams(vmem_limit_bytes=SNUG),
            cost_estimate=pl.CostEstimate(
                flops=height * across, bytes_accessed=6 * height * across, transcendentals=0
            ),
        )(state, home, new)

    new_lower = swap(lower)
    new_gate = swap(d_gate)
    d_up, new_lower = lax.optimization_barrier((d_up, new_lower))
    new_up = swap(d_up)
    block_out, d_hidden = call(
        finish_body,
        (shape((tok, width), BF16), shape((tok, width), BF16)),
        (6 * tok * width * slots, 4 * slots * width * 2),
        limit=ROOMY,
        grid=(1,),
        in_specs=[whole(back), whole(pairs), whole(combine), whole(cot), whole(hidden),
                  whole(gain), whole(w_router)],
        out_specs=(whole(cot), whole(cot)),
        scratch_shapes=[pltpu.VMEM((tok, width), F32)],
    )(back, pairs, combine, cot, hidden, gain, w_router)
    new_up, d_hidden = lax.optimization_barrier((new_up, d_hidden))
    upper, lower, d_gate, d_up = [
        widen(*pair)
        for pair in (
            (upper, new_upper), (lower, new_lower), (d_gate, new_gate), (d_up, new_up)
        )
    ]
    d_down = jnp.concatenate([upper, lower], axis=1)
    return (
        block_out.reshape(residual.shape),
        d_hidden.reshape(residual.shape),
        d_gate,
        d_up,
        d_down,
    )


def solution(mesh):
    tokens = P("frames", "expert", None)
    weights = P(("frames", "expert"), None, None)
    return jax.shard_map(
        on_device,
        mesh=mesh,
        in_specs=(tokens,) * 4
        + (P(), P(), P(), P("expert", "frames", None, None))
        + (weights,) * 3
        + (tokens,),
        out_specs=(tokens, tokens, weights, weights, weights),
        check_vma=False,
    )
```
